32 devices in a mesh: dp: 8 (over y, x, core), expert: 4 (over z).
Axes of the slice: x: 2, y: 2, z: 4, core: 2. Of those that a mesh axis runs over, the one named last changes fastest.
Arguments:
- tokens: bfloat16 [32, 512, 1536], P(('dp', 'expert')), may hold values from -6 to 6
- seq_lengths: int32 [32], P(('dp', 'expert')), may hold values from 256 to 512, as said below
- routes: int32 [32, 512, 8], P(('dp', 'expert')), may hold values from 0 to 19, all different within a row
- norm_attn: bfloat16 [1536], P('expert'), may hold values from 0.5 to 1.5
- query_key_value_weight: bfloat16 [1536, 2560], P('expert'), may hold values from -0.15625 to 0.15625
- w_out: bfloat16 [1536, 1536], P('expert'), may hold values from -1.5 to 1.5
- norm_moe: bfloat16 [1536], P('expert'), may hold values from 0.5 to 1.5
- router: bfloat16 [1536, 20], P('expert'), may hold values from -0.078125 to 0.078125
- expert_in: bfloat16 [20, 1536, 1024], P('expert', 'dp'), may hold values from -0.15625 to 0.15625
- expert_out: bfloat16 [20, 512, 1536], P('expert', 'dp'), may hold values from -1 to 1
- cotangent: bfloat16 [32, 512, 1536], P(('dp', 'expert')), may hold values from -6 to 6
Outputs:
- output: bfloat16 [32, 512, 1536], P(('dp', 'expert'))
- grad_tokens: bfloat16 [32, 512, 1536], P(('dp', 'expert'))
- grad_norm_attn: float32 [1536], P('expert')
- grad_w_qkv: float32 [1536, 2560], P('expert')
- grad_w_out: float32 [1536, 1536], P('expert')
- grad_norm_moe: float32 [1536], P('expert')
- grad_router: float32 [1536, 20], P('expert')
- grad_expert_in: float32 [20, 1536, 1024], P('expert', 'dp')
- grad_expert_out: float32 [20, 512, 1536], P('expert', 'dp')
The draws below stay inside these ranges and needn't reach their ends.
Inputs may be any that keep to these rules, and one draw needn't show every extreme that they name: `seq_lengths`: the first sequence is full.
All inputs are finite; a program needn't handle non-finite values.
Results may differ from the reference program's by a relative error of at most 0.02.
Values may be sent and summed in bfloat16 or wider, within the bound.
A program may use at most 320 MiB of HBM per device.

```python
import math
import jax
import jax.numpy as jnp
from jax import lax

MODEL_DIM = 1536
QUERY_HEADS = 24
KEY_VALUE_HEADS = 8
HEAD_SIZE = 64
H = 512
TOPK = 8
LEN = 512
SEQ_DEV = 1
EXPERTS = 20
SEQS = 32
CAP = 204


def draw_seq_lengths(key, part):
    value_rows = jax.random.randint(key, (SEQS,), LEN // 2, LEN + 1)
    return value_rows.at[0].set(LEN).astype(jnp.int32)


def steps_of(rng, shape, pieces, low, largest):
    factor_of, own = 1.0, jax.random.fold_in(rng, 6)
    for dim, shards_of in pieces:
        steps = jnp.exp(jax.random.uniform(jax.random.fold_in(own, dim), (shards_of,), jnp.float32, low / len(pieces), largest / len(pieces)))
        factor_of = factor_of * jnp.repeat(steps, shape[dim] // shards_of).reshape([-1 if axis == dim else 1 for axis in range(len(shape))])
    return factor_of


def distinct(stream_key, rows, number_of, top, lift):
    sequence = jax.random.permutation(jax.random.fold_in(stream_key, 1), number_of)
    favour = sequence
    for power in range(3):
        favour = favour * favour // number_of
    favour = favour * lift // number_of
    chance = jax.random.randint(jax.random.fold_in(stream_key, 2), (rows, number_of), 0, 4096) + favour
    holders = jax.random.permutation(jax.random.fold_in(stream_key, 3), rows)[jnp.arange(number_of) % rows]
    chance = jnp.where(jnp.arange(rows)[:, None] == holders[None, :], 1 << 14, chance)
    merit = chance * number_of + jnp.arange(number_of)
    return lax.top_k(merit.astype(jnp.int32), top)[1].astype(jnp.int32)


def gaussian(key, extent, spread, limit, pieces=(), kind=jnp.bfloat16):
    values = jax.random.normal(key, extent, jnp.float32) * spread
    if len(pieces) > 0:
        values = steps_of(key, extent, pieces, -0.22, 0.18) * values
    return jnp.clip(values, min=-limit, max=limit).astype(kind)


def setup_inputs(seed: int = 0) -> dict:
    streams_of = jax.random.split(jax.random.key(seed), 12)
    tokens = gaussian(streams_of[0], (SEQS, LEN, MODEL_DIM), 1.0, 6.0, ((0, 32),))
    seq_lengths = draw_seq_lengths(jax.random.fold_in(streams_of[11], 71), 0)
    routes = distinct(streams_of[2], SEQS * LEN, EXPERTS, TOPK, 3276).reshape((SEQS, LEN, TOPK))
    norm_attn = jnp.clip(1.0 + 0.1 * jax.random.normal(streams_of[3], (MODEL_DIM,), jnp.float32), 0.5, 1.5).astype(jnp.bfloat16)
    query_key_value_weight = gaussian(streams_of[4], (MODEL_DIM, (QUERY_HEADS + 2 * KEY_VALUE_HEADS) * HEAD_SIZE), MODEL_DIM ** -0.5, 0.15625, ((0, 4),))
    w_out = gaussian(streams_of[5], (QUERY_HEADS * HEAD_SIZE, MODEL_DIM), 16 ** -0.5, 1.5, ((0, 4),))
    norm_moe = jnp.clip(1.0 + 0.1 * jax.random.normal(streams_of[6], (MODEL_DIM,), jnp.float32), 0.5, 1.5).astype(jnp.bfloat16)
    router = gaussian(streams_of[7], (MODEL_DIM, EXPERTS), (4 * MODEL_DIM) ** -0.5, 0.078125, ((0, 4),))
    expert_in = gaussian(streams_of[8], (EXPERTS, MODEL_DIM, 2 * H), MODEL_DIM ** -0.5, 0.15625, ((0, 4), (1, 8)))
    expert_out = gaussian(streams_of[9], (EXPERTS, H, MODEL_DIM), (H // 16) ** -0.5, 1.0, ((0, 4), (1, 8)))
    cotangent = gaussian(streams_of[10], (SEQS, LEN, MODEL_DIM), 1.0, 6.0, ((0, 32),))
    return dict(tokens=tokens, seq_lengths=seq_lengths, routes=routes, norm_attn=norm_attn, query_key_value_weight=query_key_value_weight, w_out=w_out, norm_moe=norm_moe, router=router, expert_in=expert_in, expert_out=expert_out, cotangent=cotangent)


PRECISE = lax.Precision.HIGHEST
EPSILON = 1e-06
MASKED = -1000000000.0

@jax.custom_vjp
def low(v):
    return lax.optimization_barrier(v.astype(jnp.bfloat16)).astype(jnp.float32)

@jax.custom_vjp
def low_back(v):
    return v

def low_keep(v):
    return (low(v), None)

def low_pass(kept, grad):
    return (grad,)

def back_keep(v):
    return (v, None)

def back_low(kept, grad):
    return (low(grad),)
low.defvjp(low_keep, low_pass)
low_back.defvjp(back_keep, back_low)

def tables(length, head):
    half_width = head // 2
    frequency = jnp.exp(jnp.arange(half_width, dtype=jnp.float32) * (-math.log(10000.0) / half_width))
    angles = jnp.arange(length, dtype=jnp.float32)[:, None] * frequency[None, :]
    return (jnp.cos(angles), jnp.sin(angles))

def rotate(value_rows, cosine, sine_table):
    half_width = value_rows.shape[-1] // 2
    front_half = value_rows[..., :half_width]
    back_half = value_rows[..., half_width:]
    return jnp.concatenate([front_half * cosine - back_half * sine_table, back_half * cosine + front_half * sine_table], -1)

def normed(value_rows, gain_vec):
    factor = lax.rsqrt(lax.optimization_barrier(jnp.mean(value_rows * value_rows, -1, keepdims=True)) + EPSILON)
    return value_rows * factor * gain_vec

def attend(member, query_key_value_weight, cosine, sine_table):
    normed_seq, length = member
    sequence_length = normed_seq.shape[0]
    query_groups = QUERY_HEADS // KEY_VALUE_HEADS
    query_key_value_all = low_back(jnp.dot(normed_seq, query_key_value_weight, precision=PRECISE))
    query_rows = query_key_value_all[:, :QUERY_HEADS * HEAD_SIZE].reshape(sequence_length, KEY_VALUE_HEADS, query_groups, HEAD_SIZE)
    key_rows_all = query_key_value_all[:, QUERY_HEADS * HEAD_SIZE:(QUERY_HEADS + KEY_VALUE_HEADS) * HEAD_SIZE].reshape(sequence_length, KEY_VALUE_HEADS, HEAD_SIZE)
    value_rows = query_key_value_all[:, (QUERY_HEADS + KEY_VALUE_HEADS) * HEAD_SIZE:].reshape(sequence_length, KEY_VALUE_HEADS, HEAD_SIZE)
    query_rows = low(rotate(query_rows, cosine[:, None, None, :], sine_table[:, None, None, :]))
    key_rows_all = low(rotate(key_rows_all, cosine[:, None, :], sine_table[:, None, :]))
    value_rows = low(value_rows)
    scores = low_back(jnp.einsum('qgrh,kgh->grqk', query_rows, key_rows_all, precision=PRECISE) * HEAD_SIZE ** (-0.5))
    position = jnp.arange(sequence_length)
    allowed = (position[None, :] <= position[:, None]) & (position[None, :] < length)
    scores = jnp.where(allowed, scores, MASKED)
    topmost = lax.optimization_barrier(jnp.max(scores, -1, keepdims=True))
    exponent = jnp.exp(scores - topmost)
    weights = low(exponent / lax.optimization_barrier(jnp.sum(exponent, -1, keepdims=True)))
    mixed_heads = jnp.einsum('grqk,kgh->qgrh', weights, value_rows, precision=PRECISE).reshape(sequence_length, QUERY_HEADS * HEAD_SIZE)
    return low_back(low(mixed_heads))

def mixture(member, expert_in, expert_out):
    block_rows, block_weight = member
    hidden_width = expert_out.shape[1]
    copies = low_back(jnp.broadcast_to(block_rows[None], (expert_in.shape[0],) + block_rows.shape))
    projected_rows = low_back(jnp.einsum('end,edf->enf', copies, expert_in, precision=PRECISE))
    gated_rows = low(jax.nn.silu(projected_rows[..., :hidden_width]) * projected_rows[..., hidden_width:])
    returned = low_back(low(jnp.einsum('enh,ehd->end', gated_rows, expert_out, precision=PRECISE)))
    return jnp.einsum('ne,end->nd', block_weight, returned, precision=PRECISE)

def capacity_keep(seq_lengths, routes):
    blocks = SEQS // SEQ_DEV
    position = jnp.arange(LEN)
    live_tokens = position[None, :] < seq_lengths[:, None]
    live_pairs = jnp.broadcast_to(live_tokens[:, :, None], routes.shape).reshape(blocks, -1)
    chosen = routes.reshape(blocks, -1)
    onehot = (chosen[:, :, None] == jnp.arange(EXPERTS)[None, None, :]) & live_pairs[:, :, None]
    counts = onehot.astype(jnp.int32)
    before = jnp.cumsum(counts, 1) - counts
    ranking = lax.optimization_barrier(jnp.sum(before * counts, -1))
    kept_pairs = live_pairs & (ranking < CAP)
    return (kept_pairs.reshape(routes.shape), live_tokens)

def forward(tokens, norm_attn, query_key_value_weight, w_out, norm_moe, router, expert_in, expert_out, seq_lengths, routes, kept_pairs, live_tokens):
    cosine, sine_table = tables(LEN, HEAD_SIZE)
    normed_one = low(normed(tokens, norm_attn))
    attended = lax.map(jax.checkpoint(lambda member: attend(member, query_key_value_weight, cosine, sine_table)), (normed_one, seq_lengths))
    hidden_sum = tokens + low_back(jnp.einsum('sti,id->std', attended, w_out, precision=PRECISE))
    normed_two = low(normed(hidden_sum, norm_moe))
    flat_rows = normed_two.reshape(-1, MODEL_DIM)
    logits = jnp.dot(flat_rows, router, precision=PRECISE)
    flat_routes = routes.reshape(-1, TOPK)
    picked = jnp.take_along_axis(logits, flat_routes, 1)
    exponent = jnp.exp(picked - lax.optimization_barrier(jnp.max(picked, -1, keepdims=True)))
    gating = exponent / lax.optimization_barrier(jnp.sum(exponent, -1, keepdims=True))
    onehot = (flat_routes[:, :, None] == jnp.arange(EXPERTS)[None, None, :]).astype(jnp.float32)
    kept_float = kept_pairs.reshape(-1, TOPK).astype(jnp.float32)
    combine_weight = jnp.einsum('nk,nke->ne', gating * kept_float, onehot, precision=PRECISE)
    blocks = SEQS // SEQ_DEV
    mixed_rows = lax.map(jax.checkpoint(lambda member: mixture(member, expert_in, expert_out)), (flat_rows.reshape(blocks, -1, MODEL_DIM), combine_weight.reshape(blocks, -1, EXPERTS)))
    return live_tokens[:, :, None].astype(jnp.float32) * (hidden_sum + mixed_rows.reshape(tokens.shape))

def reference(tokens, seq_lengths, routes, norm_attn, query_key_value_weight, w_out, norm_moe, router, expert_in, expert_out, cotangent):
    kept_pairs, live_tokens = capacity_keep(seq_lengths, routes)
    floats = tuple((array_in.astype(jnp.float32) for array_in in (tokens, norm_attn, query_key_value_weight, w_out, norm_moe, router, expert_in, expert_out)))

    def closed(*params):
        return forward(*params, seq_lengths, routes, kept_pairs, live_tokens)
    result, pullback = jax.vjp(closed, *floats)
    gradients = pullback(cotangent.astype(jnp.float32))
    return (result.astype(jnp.bfloat16), gradients[0].astype(jnp.bfloat16), gradients[1], gradients[2], gradients[3], gradients[4], gradients[5], gradients[6], gradients[7])
```

```python
import math

import jax
import jax.numpy as jnp
from jax import lax
from jax.experimental import pallas as pl
from jax.experimental.pallas import tpu as pltpu
from jax.sharding import PartitionSpec as P

QUERY_HEADS = 24
KEY_VALUE_HEADS = 8
HEAD_SIZE = 64
TOPK = 8
AUX = 128

PRECISE = lax.Precision.HIGHEST
EPSILON = 1e-06
MASKED = -1000000000.0
F32 = jnp.float32
BF16 = jnp.bfloat16


def tables(length, head):
    half_width = head // 2
    frequency = jnp.exp(jnp.arange(half_width, dtype=F32) * (-math.log(10000.0) / half_width))
    angles = jnp.arange(length, dtype=F32)[:, None] * frequency[None, :]
    return (jnp.cos(angles), jnp.sin(angles))


def rotate(value_rows, cosine, sine_table):
    half_width = value_rows.shape[-1] // 2
    front_half = value_rows[..., :half_width]
    back_half = value_rows[..., half_width:]
    return jnp.concatenate(
        [
            front_half * cosine - back_half * sine_table,
            back_half * cosine + front_half * sine_table,
        ],
        -1,
    )


def norm_apply(value_rows, gain_vec):
    factor = lax.rsqrt(jnp.mean(value_rows * value_rows, -1, keepdims=True) + EPSILON)
    return (value_rows * factor * gain_vec, factor)


def norm_back(value_rows, factor, gain_vec, incoming):
    unit_rows = value_rows * factor
    scaled = incoming * gain_vec
    gain_grad = jnp.sum(incoming * unit_rows, 0)
    return (
        factor * (scaled - unit_rows * jnp.mean(scaled * unit_rows, -1, keepdims=True)),
        gain_grad,
    )


def dot(spec, a, b):
    return jnp.einsum(spec, a, b, preferred_element_type=F32)


def masked_scores(query_rows, key_rows_all, length, scale_factor):
    sequence_length = query_rows.shape[0]
    scores = dot("qgrh,kgh->grqk", query_rows, key_rows_all) * scale_factor
    position = jnp.arange(sequence_length)
    allowed = (position[None, :] <= position[:, None]) & (position[None, :] < length)
    return jnp.where(allowed, scores, MASKED)


def attend_forward(query_rows, key_rows_all, value_rows, length, scale_factor):
    scores = masked_scores(query_rows, key_rows_all, length, scale_factor)
    topmost = jnp.max(scores, -1, keepdims=True)
    exponent = jnp.exp(scores - topmost)
    totals = jnp.sum(exponent, -1, keepdims=True)
    weights = (exponent / totals).astype(BF16)
    mixed_heads = dot("grqk,kgh->qgrh", weights, value_rows)
    return (
        mixed_heads.astype(BF16).reshape(query_rows.shape[0], -1),
        topmost + jnp.log(totals),
    )


def attend_backward(query_rows, key_rows_all, value_rows, length, log_total, upstream, scale_factor):
    scores = masked_scores(query_rows, key_rows_all, length, scale_factor)
    weights = jnp.exp(scores - log_total)
    upstream_heads = upstream.reshape(query_rows.shape)
    weight_grad = dot("qgrh,kgh->grqk", upstream_heads, value_rows)
    score_grad = (
        weights * (weight_grad - jnp.sum(weights * weight_grad, -1, keepdims=True))
    ).astype(BF16)
    query_grad = dot("grqk,kgh->qgrh", score_grad, key_rows_all) * scale_factor
    key_grad = dot("grqk,qgrh->kgh", score_grad, query_rows) * scale_factor
    value_grad = dot("grqk,qgrh->kgh", weights.astype(BF16), upstream_heads)
    return (query_grad, key_grad, value_grad)


def split_two(values):
    high = values.astype(BF16)
    low = (values - high.astype(F32)).astype(BF16)
    return (high, low)


MESH = pl.DeviceIdType.MESH
VMEM_LIMIT = 60 * 1024 * 1024


def vmem_spec():
    return pl.BlockSpec(memory_space=pltpu.VMEM)


def any_spec():
    return pl.BlockSpec(memory_space=pl.ANY)


def kernel_params(collective):
    return pltpu.CompilerParams(
        collective_id=collective, has_side_effects=True, vmem_limit_bytes=VMEM_LIMIT
    )


def greet_all(me, owners, dp_index, bits):
    barrier = pltpu.get_barrier_semaphore()
    for bit in range(bits):
        pl.semaphore_signal(
            barrier, inc=1, device_id={"dp": partner_of(dp_index, bit)}, device_id_type=MESH
        )
    ends = (me > 0, me < owners - 1)
    for offset, there in zip((-1, 1), ends):

        @pl.when(there)
        def _():
            pl.semaphore_signal(
                barrier, inc=1, device_id={"expert": me + offset}, device_id_type=MESH
            )

    pl.semaphore_wait(barrier, bits + ends[0].astype(jnp.int32) + ends[1].astype(jnp.int32))


def bit_of(index, bit):
    return lax.rem(index // (1 << bit), 2)


def partner_of(index, bit):
    return index + (1 - 2 * bit_of(index, bit)) * (1 << bit)


def line_sends(me, owners, source_of, target_of, send, recv, slot):
    first = []
    for side in range(2):
        toward = 1 - 2 * side
        behind = me if side == 0 else owners - 1 - me

        def copy(step, side=side, toward=toward):
            origin = me - toward * step
            return pltpu.make_async_remote_copy(
                src_ref=source_of(step, origin),
                dst_ref=target_of(origin),
                send_sem=send.at[slot, side, step],
                recv_sem=recv.at[slot, side, step],
                device_id={"expert": me + toward},
                device_id_type=MESH,
            )

        first.append((behind, copy))
    return first


def line_step(step, sides, owners):
    for behind, copy in sides:
        if step > 0:

            @pl.when(behind >= step)
            def _():
                copy(step - 1).wait_recv()

        if step < owners - 1:

            @pl.when((behind >= step) & (behind < owners - 1))
            def _():
                copy(step).start()


def line_finish(sides, owners):
    for behind, copy in sides:
        for step in range(owners - 1):

            @pl.when((behind >= step) & (behind < owners - 1))
            def _():
                copy(step).wait_send()


def line_gather(blocks, owners, collective):
    count = len(blocks)

    def kernel(*refs):
        own, outs = refs[:count], refs[count : 2 * count]
        send, recv, local = refs[2 * count :]
        me = lax.axis_index("expert")
        greet_all(me, owners, 0, 0)
        lines, copies = [], []
        for i in range(count):

            def source_of(step, origin, i=i):
                return own[i] if step == 0 else outs[i].at[origin]

            def target_of(origin, i=i):
                return outs[i].at[origin]

            lines.append(line_sends(me, owners, source_of, target_of, send, recv, i))
        for step in range(owners):
            for i in range(count):
                line_step(step, lines[i], owners)
            if step == 0:
                for i in range(count):
                    copies.append(pltpu.make_async_copy(own[i], outs[i].at[me], local.at[i]))
                    copies[-1].start()
        for i in range(count):
            copies[i].wait()
            line_finish(lines[i], owners)

    return pl.pallas_call(
        kernel,
        out_shape=[jax.ShapeDtypeStruct((owners,) + b.shape, b.dtype) for b in blocks],
        in_specs=[vmem_spec()] * count,
        out_specs=[any_spec()] * count,
        scratch_shapes=[
            pltpu.SemaphoreType.DMA((count, 2, owners - 1)),
            pltpu.SemaphoreType.DMA((count, 2, owners - 1)),
            pltpu.SemaphoreType.DMA((count,)),
        ],
        compiler_params=kernel_params(collective),
    )(*blocks)


def add_rows(target, addend, chunk):
    @pl.loop(0, target.shape[0] // chunk)
    def _(index):
        rows = pl.ds(pl.multiple_of(index * chunk, chunk), chunk)
        target[rows, :] = (target[rows, :].astype(F32) + addend[rows, :].astype(F32)).astype(
            target.dtype
        )


def scatter_line(own, held, out, send, recv, me, owners, chunk):
    def copy(side, step, source):
        toward = 1 - 2 * side
        return pltpu.make_async_remote_copy(
            src_ref=source,
            dst_ref=held.at[side, step],
            send_sem=send.at[side, step],
            recv_sem=recv.at[side, step],
            device_id={"expert": me + toward},
            device_id_type=MESH,
        )

    def advance(step):
        for side in range(2):
            toward = 1 - 2 * side
            behind = me if side == 0 else owners - 1 - me
            block = own.at[me + toward * (owners - 1 - step)]

            @pl.when(behind == 0)
            def _():
                copy(side, step, block).start()

            if step > 0:
                before = held.at[side, step - 1]

                @pl.when((behind >= 1) & (behind <= step))
                def _():
                    copy(side, step - 1, before).wait_recv()
                    add_rows(before, block, chunk)
                    copy(side, step, before).start()

    def finish():
        for side in range(2):
            behind = me if side == 0 else owners - 1 - me

            @pl.when(behind >= 1)
            def _():
                copy(side, owners - 2, held.at[side, owners - 2]).wait_recv()

        right, left = held.at[0, owners - 2], held.at[1, owners - 2]
        mine = own.at[me]

        @pl.loop(0, out.shape[0] // chunk)
        def _(index):
            rows = pl.ds(pl.multiple_of(index * chunk, chunk), chunk)
            total = mine[rows, :].astype(F32)
            zero = jnp.zeros_like(total)
            total = total + jnp.where(me > 0, right[rows, :].astype(F32), zero)
            total = total + jnp.where(me < owners - 1, left[rows, :].astype(F32), zero)
            out[rows, :] = total.astype(out.dtype)

        for side in range(2):
            behind = me if side == 0 else owners - 1 - me
            for step in range(owners - 1):

                @pl.when(behind <= step)
                def _():
                    copy(side, step, held.at[side, step]).wait_send()

    return advance, finish


def line_scratch(block, owners):
    return [
        pltpu.VMEM((2, owners - 1) + block.shape[1:], block.dtype),
        pltpu.SemaphoreType.DMA((2, owners - 1)),
        pltpu.SemaphoreType.DMA((2, owners - 1)),
    ]


def line_scatter(blocks, owners, collective):
    count = len(blocks)

    def kernel(*refs):
        own, outs, scratch = refs[:count], refs[count : 2 * count], refs[2 * count :]
        me = lax.axis_index("expert")
        greet_all(me, owners, 0, 0)
        lines = []
        for i in range(count):
            held, send, recv = scratch[3 * i : 3 * i + 3]
            lines.append(scatter_line(own[i], held, outs[i], send, recv, me, owners, 32))
        for step in range(owners - 1):
            for advance, _ in lines:
                advance(step)
        for _, finish in lines:
            finish()

    return pl.pallas_call(
        kernel,
        out_shape=[jax.ShapeDtypeStruct(b.shape[1:], F32) for b in blocks],
        in_specs=[vmem_spec()] * count,
        out_specs=[vmem_spec()] * count,
        scratch_shapes=[one for b in blocks for one in line_scratch(b, owners)],
        compiler_params=kernel_params(collective),
    )(*blocks)


def column_parts(width):
    middle = width // 2 // 128 * 128
    return ((0, middle), (middle, width))


def bit_order(part, bits):
    return list(range(1, bits)) if part == 0 else list(range(bits - 1, 0, -1))


def spread(out, place, start, stop):
    return out.at[tuple(place) + (slice(None), slice(start, stop))]


def fan_out(arrays, lead, dp_index, bits, send, recv):
    def copy(slot, ref, bit, known, start, stop):
        place = lead + [
            slice(None) if one in known else bit_of(dp_index, one)
            for one in range(bits - 1, -1, -1)
        ]
        view = ref.at[tuple(place) + (slice(None), slice(start, stop))]
        return pltpu.make_async_remote_copy(
            src_ref=view,
            dst_ref=view,
            send_sem=send.at[slot],
            recv_sem=recv.at[slot],
            device_id={"dp": partner_of(dp_index, bit)},
            device_id_type=MESH,
        )

    slot = 0
    for stage in range(bits):
        going = []
        for ref in arrays:
            if stage == bits - 1:
                going.append(copy(slot, ref, 0, set(range(1, bits)), 0, ref.shape[-1]))
                slot += 1
                continue
            for part, (start, stop) in enumerate(column_parts(ref.shape[-1])):
                order = bit_order(part, bits)
                going.append(
                    copy(slot, ref, order[stage], set(order[:stage]), start, stop)
                )
                slot += 1
        for one in going:
            one.start()
        for one in going:
            one.wait()


def reduce_all(grads, blocks, owners, dp_size, collective):
    bits = dp_size.bit_length() - 1
    shapes = [(g.shape[0] // (owners * dp_size), g.shape[1]) for g in grads]
    count, extra = len(grads), len(blocks)
    pieces = [
        (i, part, start, stop)
        for i, (_, width) in enumerate(shapes)
        for part, (start, stop) in enumerate(column_parts(width))
    ]
    many = len(pieces)

    def kernel(*refs):
        take = iter(refs)
        grad_refs = [next(take) for _ in range(count)]
        block_refs = [next(take) for _ in range(extra)]
        outs = [next(take) for _ in range(count)]
        block_outs = [next(take) for _ in range(extra)]
        pairs = [next(take) for _ in range(count)]
        held = [[next(take) for _ in range(many)] for _ in range(bits - 1)]
        small = [[next(take) for _ in range(3)] for _ in range(many)]
        large = [[next(take) for _ in range(3)] for _ in range(extra)]
        fold_send, fold_recv, fan_send, fan_recv = take
        me, dp_index = lax.axis_index("expert"), lax.axis_index("dp")
        greet_all(me, owners, dp_index, bits)
        lines = [
            scatter_line(block_refs[i], large[i][0], block_outs[i], *large[i][1:], me, owners, 32)
            for i in range(extra)
        ]
        pending = [0]

        def push_lines():
            step = pending[0]
            pending[0] += 1
            for advance, finish in lines:
                if step < owners - 1:
                    advance(step)
                elif step == owners - 1:
                    finish()

        def fold(slot, bit, source, target):
            return pltpu.make_async_remote_copy(
                src_ref=source,
                dst_ref=target,
                send_sem=fold_send.at[slot],
                recv_sem=fold_recv.at[slot],
                device_id={"dp": partner_of(dp_index, bit)},
                device_id_type=MESH,
            )

        def add_all(target, source_of):
            others = list(target.shape[1:-2])

            @pl.loop(0, owners)
            def _(z):
                for flat in range(math.prod(others)):
                    place, rest = [], flat
                    for size in reversed(others):
                        place.insert(0, rest % size)
                        rest //= size
                    index = (z,) + tuple(place)
                    target[index] = (
                        target[index].astype(F32) + source_of(z, place).astype(F32)
                    ).astype(target.dtype)

        mine = bit_of(dp_index, 0)
        going = []
        for i in range(count):
            source = grad_refs[i].at[(slice(None),) * bits + (1 - mine,)]
            going.append(fold(i, 0, source, pairs[i]))
            going[-1].start()
        push_lines()
        for i in range(count):
            going[i].wait()
            add_all(pairs[i], lambda z, place: grad_refs[i][(z,) + tuple(place) + (mine,)])
        state = []
        for i, part, start, stop in pieces:
            columns = slice(start, stop)
            state.append((pairs[i], columns, sorted(range(1, bits), reverse=True)))
        for stage in range(bits - 1):
            going = []
            for index, (i, part, start, stop) in enumerate(pieces):
                ref, columns, axes = state[index]
                bit = bit_order(part, bits)[stage]
                axis = axes.index(bit)
                view = (slice(None),) * (1 + axis) + (1 - bit_of(dp_index, bit),)
                view = view + (slice(None),) * (len(axes) - axis) + (columns,)
                target = held[stage][index]
                one = fold(count + stage * many + index, bit, ref.at[view], target)
                one.start()
                going.append((one, target, ref, axis, bit, columns, axes))
            for index, (one, target, ref, axis, bit, columns, axes) in enumerate(going):
                one.wait()
                keep = bit_of(dp_index, bit)

                def source_of(z, place):
                    where = (z,) + tuple(place[:axis]) + (keep,) + tuple(place[axis:])
                    return ref[where + (slice(None), columns)]

                add_all(target, source_of)
                state[index] = (target, slice(None), [a for a in axes if a != bit])
            if stage == 0:
                push_lines()

        place = tuple(bit_of(dp_index, bit) for bit in range(bits - 1, -1, -1))
        short = []
        for index, (i, part, start, stop) in enumerate(pieces):
            rows = shapes[i][0]
            target = outs[i].at[place + (slice(None), slice(start, stop))]
            short.append(
                scatter_line(
                    state[index][0], small[index][0], target, *small[index][1:], me, owners, rows
                )
            )
        for step in range(owners - 1):
            for advance, _ in short:
                advance(step)
        for _, finish in short:
            finish()
        push_lines()
        fan_out(outs, [], dp_index, bits, fan_send, fan_recv)
        while pending[0] < owners:
            push_lines()

    scratch = []
    for rows, width in shapes:
        scratch.append(pltpu.VMEM((owners,) + (2,) * (bits - 1) + (rows, width), BF16))
    for stage in range(bits - 1):
        for i, part, start, stop in pieces:
            scratch.append(
                pltpu.VMEM(
                    (owners,) + (2,) * (bits - 2 - stage) + (shapes[i][0], stop - start), BF16
                )
            )
    for i, part, start, stop in pieces:
        block = jax.ShapeDtypeStruct((owners, shapes[i][0], stop - start), BF16)
        scratch += line_scratch(block, owners)
    for block in blocks:
        scratch += line_scratch(block, owners)
    folds = count + (bits - 1) * many
    fans = count + (bits - 1) * many
    scratch += [pltpu.SemaphoreType.DMA((folds,))] * 2 + [pltpu.SemaphoreType.DMA((fans,))] * 2
    operands = [
        g.reshape((owners,) + (2,) * bits + shape) for g, shape in zip(grads, shapes)
    ] + list(blocks)
    results = pl.pallas_call(
        kernel,
        out_shape=[jax.ShapeDtypeStruct((2,) * bits + shape, BF16) for shape in shapes]
        + [jax.ShapeDtypeStruct(b.shape[1:], F32) for b in blocks],
        in_specs=[vmem_spec()] * len(operands),
        out_specs=[vmem_spec()] * len(operands),
        scratch_shapes=scratch,
        compiler_params=kernel_params(collective),
    )(*operands)
    sums = [
        r.reshape(dp_size * rows, width) for r, (rows, width) in zip(results, shapes)
    ]
    return sums, results[count:]


def gather_rows(piece, block, owners, dp_size, collective):
    bits = dp_size.bit_length() - 1
    rows, width = piece.shape[0] // dp_size, piece.shape[1]
    shape = (owners,) + (2,) * bits + (rows, width)

    def kernel(piece_ref, block_ref, out, near, *scratch):
        line_send, line_recv, near_send, near_recv, fan_send, fan_recv, local = scratch
        me, dp_index = lax.axis_index("expert"), lax.axis_index("dp")
        greet_all(me, owners, dp_index, bits)
        place = tuple(bit_of(dp_index, bit) for bit in range(bits - 1, -1, -1))
        mine = piece_ref.at[place]

        def source_of(step, origin):
            return mine if step == 0 else out.at[(origin,) + place]

        def target_of(origin):
            return out.at[(origin,) + place]

        sides = line_sends(me, owners, source_of, target_of, line_send, line_recv, 0)
        keep = pltpu.make_async_copy(mine, out.at[(me,) + place], local)
        for step in range(owners):
            line_step(step, sides, owners)
            if step == 0:
                keep.start()
        keep.wait()

        def nearby(side):
            return pltpu.make_async_remote_copy(
                src_ref=block_ref,
                dst_ref=near.at[side],
                send_sem=near_send.at[side],
                recv_sem=near_recv.at[side],
                device_id={"expert": me + 1 - 2 * side},
                device_id_type=MESH,
            )

        ahead = (owners - 1 - me, me)
        for side in range(2):

            @pl.when(ahead[side] > 0)
            def _():
                nearby(side).start()

        fan_out([out], [slice(None)], dp_index, bits, fan_send, fan_recv)
        line_finish(sides, owners)
        for side in range(2):

            @pl.when(ahead[side] > 0)
            def _():
                nearby(side).wait_send()

            @pl.when(ahead[1 - side] > 0)
            def _():
                nearby(side).wait_recv()

    full, near = pl.pallas_call(
        kernel,
        out_shape=[
            jax.ShapeDtypeStruct(shape, BF16),
            jax.ShapeDtypeStruct((2,) + block.shape, BF16),
        ],
        in_specs=[vmem_spec()] * 2,
        out_specs=[any_spec()] * 2,
        scratch_shapes=[
            pltpu.SemaphoreType.DMA((1, 2, owners - 1)),
            pltpu.SemaphoreType.DMA((1, 2, owners - 1)),
            pltpu.SemaphoreType.DMA((2,)),
            pltpu.SemaphoreType.DMA((2,)),
            pltpu.SemaphoreType.DMA((2 * bits - 1,)),
            pltpu.SemaphoreType.DMA((2 * bits - 1,)),
            pltpu.SemaphoreType.DMA,
        ],
        compiler_params=kernel_params(collective),
    )(piece.reshape((2,) * bits + (rows, width)), block)
    return full.reshape(owners * dp_size * rows, width), near


def permute_gather(block, near, owner, owners):
    right, left = near[0], near[1]
    rightward, leftward = [right], [left]
    for step in range(1, owners - 1):
        right = lax.ppermute(right, "expert", [(z, z + 1) for z in range(step, owners - 1)])
        left = lax.ppermute(left, "expert", [(z, z - 1) for z in range(1, owners - step)])
        rightward.append(right)
        leftward.append(left)
    blocks = [block] + [
        jnp.where(owner + k < owners, leftward[k - 1], rightward[owners - k - 1])
        for k in range(1, owners)
    ]
    whole = jnp.concatenate(blocks + blocks, 0)
    return lax.dynamic_slice_in_dim(
        whole, lax.rem(owners - owner, owners) * block.shape[0], owners * block.shape[0], 0
    ).reshape((owners,) + block.shape)


def gather_slow(piece, dp_index, dp_size):
    rows = piece.shape[0] // dp_size
    part = lax.dynamic_slice_in_dim(piece, dp_index * rows, rows, 0)
    return lax.all_gather(part, ("expert", "dp"), axis=0, tiled=True)


def per_device(
    tokens,
    seq_lengths,
    routes,
    norm_attn,
    query_key_value_weight,
    w_out,
    norm_moe,
    router,
    expert_in,
    expert_out,
    cotangent,
):
    owners = lax.axis_size("expert")
    dp_size = lax.axis_size("dp")
    owner = lax.axis_index("expert")
    dp_index = lax.axis_index("dp")
    _, length, width = tokens.shape
    query_groups = QUERY_HEADS // KEY_VALUE_HEADS
    local_experts = expert_in.shape[0]
    experts = local_experts * owners
    capacity = length * TOPK // experts
    scale_factor = HEAD_SIZE ** (-0.5)
    query_width = QUERY_HEADS * HEAD_SIZE
    key_width = KEY_VALUE_HEADS * HEAD_SIZE
    qkv_width = query_width + 2 * key_width

    small = jnp.concatenate(
        [
            router,
            norm_attn[:, None],
            norm_moe[:, None],
            jnp.zeros((router.shape[0], AUX - experts - 2), BF16),
        ],
        1,
    )
    qkv_packed, near = gather_rows(
        jnp.concatenate([query_key_value_weight, small], 1), cotangent[0], owners, dp_size, 1
    )
    out_full = gather_slow(w_out, dp_index, dp_size)
    upstream_all = permute_gather(cotangent[0], near, owner, owners)
    small_full = qkv_packed[:, qkv_width:].astype(F32)
    router_wide = small_full[:, :experts]
    gain_first = small_full[:, experts]
    gain_second = small_full[:, experts + 1]

    sequence_live = seq_lengths[0]
    position = jnp.arange(length)
    live = position < sequence_live
    live_rows = live[:, None].astype(F32)
    inputs = tokens[0].astype(F32)
    normed_first, factor_first = norm_apply(inputs, gain_first)
    normed_low = normed_first.astype(BF16)
    projected_rows = dot("td,df->tf", normed_low, qkv_packed)
    cosine, sine_table = tables(length, HEAD_SIZE)
    cos_four = cosine[:, None, None, :]
    sin_four = sine_table[:, None, None, :]
    cos_three = cosine[:, None, :]
    sin_three = sine_table[:, None, :]
    query_rows = rotate(
        projected_rows[:, :query_width].reshape(length, KEY_VALUE_HEADS, query_groups, HEAD_SIZE),
        cos_four,
        sin_four,
    ).astype(BF16)
    key_rows_all = rotate(
        projected_rows[:, query_width : query_width + key_width].reshape(
            length, KEY_VALUE_HEADS, HEAD_SIZE
        ),
        cos_three,
        sin_three,
    ).astype(BF16)
    value_rows = (
        projected_rows[:, query_width + key_width : qkv_width]
        .reshape(length, KEY_VALUE_HEADS, HEAD_SIZE)
        .astype(BF16)
    )
    attended, log_total = attend_forward(
        query_rows, key_rows_all, value_rows, sequence_live, scale_factor
    )
    hidden_sum = inputs + dot("ti,id->td", attended, out_full)
    normed_second, factor_second = norm_apply(hidden_sum, gain_second)
    second_low = normed_second.astype(BF16)

    chosen = jnp.any(routes[0][:, :, None] == jnp.arange(experts)[None, None, :], 1)
    pairs = chosen & live[:, None]
    earlier = (position[:, None] > position[None, :]).astype(BF16)
    ranking = dot("tu,ue->te", earlier, pairs.astype(BF16))
    kept = pairs & (ranking < capacity)
    logits = jnp.dot(second_low.astype(F32), router_wide, precision=PRECISE)
    topmost = jnp.max(jnp.where(chosen, logits, -jnp.inf), -1, keepdims=True)
    exponent = jnp.where(chosen, jnp.exp(jnp.where(chosen, logits - topmost, 0.0)), 0.0)
    gating = exponent / jnp.sum(exponent, -1, keepdims=True)
    kept_weight = jnp.where(kept, gating, 0.0)
    slot_of = jnp.where(kept, ranking, -1.0).astype(BF16)
    weight_high, weight_low = split_two(kept_weight)
    extra = jnp.concatenate(
        [slot_of, weight_high, weight_low, jnp.zeros((length, AUX - 3 * experts), BF16)], 1
    )
    rows_all, extra_all = line_gather([second_low, extra], owners, 2)
    extra_all = extra_all.astype(F32)

    def own(column):
        return lax.dynamic_slice_in_dim(
            extra_all, column * experts + owner * local_experts, local_experts, 2
        )

    slots = own(0)
    weights_all = own(1) + own(2)
    hits = slots.transpose(0, 2, 1)[:, :, None, :] == jnp.arange(capacity, dtype=F32)[:, None]
    picks = hits.astype(BF16)
    slot_weight = jnp.sum(
        jnp.where(hits, weights_all.transpose(0, 2, 1)[:, :, None, :], 0.0), -1
    )
    inner_full = lax.all_gather(expert_in, "dp", axis=1, tiled=True)
    down_full = lax.all_gather(expert_out, "dp", axis=1, tiled=True)
    hidden_width = down_full.shape[1]

    rows_in = dot("sect,std->escd", picks, rows_all).astype(BF16)
    grad_in = dot("sect,std->escd", picks, upstream_all).astype(BF16)
    gate_up = dot("escd,edf->escf", rows_in, inner_full)
    gate_part = gate_up[..., :hidden_width]
    up_part = gate_up[..., hidden_width:]
    sigmoid_part = jax.nn.sigmoid(gate_part)
    activated = gate_part * sigmoid_part
    hidden = activated * up_part
    weight_column = slot_weight.transpose(1, 0, 2)[..., None]
    hidden_weighted = (hidden * weight_column).astype(BF16)
    hidden_grad = dot("escd,ehd->esch", grad_in, down_full)
    gate_grad_slot = jnp.sum(hidden.astype(BF16).astype(F32) * hidden_grad, -1)
    hidden_grad = hidden_grad * weight_column
    gate_part_grad = hidden_grad * up_part * sigmoid_part * (1.0 + gate_part * (1.0 - sigmoid_part))
    up_grad = hidden_grad * activated
    gate_up_grad = jnp.concatenate([gate_part_grad, up_grad], -1).astype(BF16)
    row_grad = dot("escf,edf->escd", gate_up_grad, inner_full).astype(BF16)
    back = dot("sect,escd->std", picks, row_grad).astype(BF16)
    gate_grad_own = jnp.sum(
        jnp.where(hits, gate_grad_slot.transpose(1, 0, 2)[..., None], 0.0), 2
    ).transpose(0, 2, 1)
    gate_wide = jnp.zeros((owners, length, experts), F32)
    gate_wide = lax.dynamic_update_slice_in_dim(gate_wide, gate_grad_own, owner * local_experts, 2)
    gate_packed = jnp.concatenate(
        list(split_two(gate_wide)) + [jnp.zeros((owners, length, AUX - 2 * experts), BF16)], 2
    )
    inner_weight_grad = dot("escd,escf->edf", rows_in, gate_up_grad).astype(BF16)
    down_weight_grad = dot("esch,escd->ehd", hidden_weighted, grad_in).astype(BF16)
    back, inner_weight_grad, down_weight_grad = lax.optimization_barrier(
        (back, inner_weight_grad, down_weight_grad)
    )
    inner_sum = lax.psum_scatter(
        inner_weight_grad, "dp", scatter_dimension=1, tiled=True
    ).astype(F32)
    down_sum = lax.psum_scatter(
        down_weight_grad, "dp", scatter_dimension=1, tiled=True
    ).astype(F32)
    back_sum, gate_sum = line_scatter([back, gate_packed], owners, 3)
    back_sum, hidden_late = lax.optimization_barrier((back_sum, hidden_weighted))
    expert_rows = dot("esch,ehd->escd", hidden_late, down_full).astype(BF16)
    mixed = dot("sect,escd->std", picks, expert_rows).astype(BF16)

    upstream = cotangent[0].astype(F32) * live_rows
    gate_grad = gate_sum[:, :experts] + gate_sum[:, experts : 2 * experts]
    logit_grad = gating * (gate_grad - jnp.sum(gating * gate_grad, -1, keepdims=True))
    second_grad = back_sum + jnp.dot(
        logit_grad, router_wide.T, precision=PRECISE
    )
    router_grad = jnp.dot(second_low.astype(F32).T, logit_grad, precision=PRECISE)
    hidden_back, gain_two_grad = norm_back(hidden_sum, factor_second, gain_second, second_grad)
    total_grad = upstream + hidden_back
    total_low = total_grad.astype(BF16)
    out_weight_grad = dot("ti,td->id", attended, total_low)
    attended_grad = dot("td,id->ti", total_low, out_full).astype(BF16)
    query_grad, key_grad, value_grad = attend_backward(
        query_rows, key_rows_all, value_rows, sequence_live, log_total, attended_grad, scale_factor
    )
    query_grad = rotate(query_grad, cos_four, -sin_four)
    key_grad = rotate(key_grad, cos_three, -sin_three)
    projected_grad = jnp.concatenate(
        [
            query_grad.reshape(length, -1),
            key_grad.reshape(length, -1),
            value_grad.reshape(length, -1),
            jnp.zeros((length, AUX), F32),
        ],
        -1,
    ).astype(BF16)
    qkv_weight_grad = dot("td,tf->df", normed_low, projected_grad)
    first_grad = dot("tf,df->td", projected_grad, qkv_packed)
    input_back, gain_one_grad = norm_back(inputs, factor_first, gain_first, first_grad)
    input_grad = (total_grad + input_back).astype(BF16)
    small_grad = jnp.concatenate(
        [
            router_grad,
            gain_one_grad[:, None],
            gain_two_grad[:, None],
            jnp.zeros((width, AUX - experts - 2), F32),
        ],
        1,
    )
    packed_grad = lax.dynamic_update_slice(
        qkv_weight_grad.astype(BF16), small_grad.astype(BF16), (0, qkv_width)
    )
    grads = [packed_grad, out_weight_grad.astype(BF16)]
    if owners > 4:
        (packed_sum, out_sum), _ = reduce_all(grads, [], owners, dp_size, 4)
        (mixture,) = line_scatter([mixed], owners, 5)
    else:
        (packed_sum, out_sum), (mixture,) = reduce_all(grads, [mixed], owners, dp_size, 4)
    packed_sum = packed_sum.astype(F32)
    output = (live_rows * (hidden_sum + mixture)).astype(BF16)
    return (
        output[None],
        input_grad[None],
        packed_sum[:, qkv_width + experts],
        packed_sum[:, :qkv_width],
        out_sum.astype(F32),
        packed_sum[:, qkv_width + experts + 1],
        packed_sum[:, qkv_width : qkv_width + experts],
        inner_sum,
        down_sum,
    )


def solution(mesh):
    return jax.shard_map(
        per_device,
        mesh=mesh,
        in_specs=(
            P(("dp", "expert"), None, None),
            P(("dp", "expert")),
            P(("dp", "expert"), None, None),
            P("expert"),
            P("expert", None),
            P("expert", None),
            P("expert"),
            P("expert", None),
            P("expert", "dp", None),
            P("expert", "dp", None),
            P(("dp", "expert"), None, None),
        ),
        out_specs=(
            P(("dp", "expert"), None, None),
            P(("dp", "expert"), None, None),
            P("expert"),
            P("expert", None),
            P("expert", None),
            P("expert"),
            P("expert", None),
            P("expert", "dp", None),
            P("expert", "dp", None),
        ),
        check_vma=False,
    )
```

```python
import math

import jax
import jax.numpy as jnp
from jax import lax
from jax.experimental import pallas as pl
from jax.experimental.pallas import tpu as pltpu
from jax.sharding import PartitionSpec as P

QUERY_HEADS = 24
KEY_VALUE_HEADS = 8
HEAD_SIZE = 64
TOPK = 8
AUX = 128

PRECISE = lax.Precision.HIGHEST
EPSILON = 1e-06
MASKED = -1000000000.0
F32 = jnp.float32
BF16 = jnp.bfloat16


def tables(length, head):
    half_width = head // 2
    frequency = jnp.exp(jnp.arange(half_width, dtype=F32) * (-math.log(10000.0) / half_width))
    angles = jnp.arange(length, dtype=F32)[:, None] * frequency[None, :]
    return (jnp.cos(angles), jnp.sin(angles))


def norm_apply(value_rows, gain_vec):
    factor = lax.rsqrt(jnp.mean(value_rows * value_rows, -1, keepdims=True) + EPSILON)
    return (value_rows * factor * gain_vec, factor)


def norm_back(value_rows, factor, gain_vec, incoming):
    unit_rows = value_rows * factor
    scaled = incoming * gain_vec
    gain_grad = jnp.sum(incoming * unit_rows, 0)
    return (
        factor * (scaled - unit_rows * jnp.mean(scaled * unit_rows, -1, keepdims=True)),
        gain_grad,
    )


def dot(spec, a, b):
    return jnp.einsum(spec, a, b, preferred_element_type=F32)


def split_two(values):
    high = values.astype(BF16)
    low = (values - high.astype(F32)).astype(BF16)
    return (high, low)


MESH = pl.DeviceIdType.MESH
VMEM_LIMIT = 60 * 1024 * 1024


def vmem_spec():
    return pl.BlockSpec(memory_space=pltpu.VMEM)


def any_spec():
    return pl.BlockSpec(memory_space=pl.ANY)


def kernel_params(collective):
    return pltpu.CompilerParams(
        collective_id=collective, has_side_effects=True, vmem_limit_bytes=VMEM_LIMIT
    )


def greet_all(me, owners, dp_index, bits):
    barrier = pltpu.get_barrier_semaphore()
    for bit in range(bits):
        pl.semaphore_signal(
            barrier, inc=1, device_id={"dp": partner_of(dp_index, bit)}, device_id_type=MESH
        )
    ends = (me > 0, me < owners - 1)
    for offset, there in zip((-1, 1), ends):

        @pl.when(there)
        def _():
            pl.semaphore_signal(
                barrier, inc=1, device_id={"expert": me + offset}, device_id_type=MESH
            )

    pl.semaphore_wait(barrier, bits + ends[0].astype(jnp.int32) + ends[1].astype(jnp.int32))


def bit_of(index, bit):
    return lax.rem(index // (1 << bit), 2)


def partner_of(index, bit):
    return index + (1 - 2 * bit_of(index, bit)) * (1 << bit)


def line_sends(me, owners, source_of, target_of, send, recv, slot):
    first = []
    for side in range(2):
        toward = 1 - 2 * side
        behind = me if side == 0 else owners - 1 - me

        def copy(step, side=side, toward=toward):
            origin = me - toward * step
            return pltpu.make_async_remote_copy(
                src_ref=source_of(step, origin),
                dst_ref=target_of(origin),
                send_sem=send.at[slot, side, step],
                recv_sem=recv.at[slot, side, step],
                device_id={"expert": me + toward},
                device_id_type=MESH,
            )

        first.append((behind, copy))
    return first


def line_step(step, sides, owners):
    for behind, copy in sides:
        if step > 0:

            @pl.when(behind >= step)
            def _():
                copy(step - 1).wait_recv()

        if step < owners - 1:

            @pl.when((behind >= step) & (behind < owners - 1))
            def _():
                copy(step).start()


def line_finish(sides, owners):
    for behind, copy in sides:
        for step in range(owners - 1):

            @pl.when((behind >= step) & (behind < owners - 1))
            def _():
                copy(step).wait_send()


def line_gather(blocks, owners, collective):
    count = len(blocks)

    def kernel(*refs):
        own, outs = refs[:count], refs[count : 2 * count]
        send, recv, local = refs[2 * count :]
        me = lax.axis_index("expert")
        greet_all(me, owners, 0, 0)
        lines, copies = [], []
        for i in range(count):

            def source_of(step, origin, i=i):
                return own[i] if step == 0 else outs[i].at[origin]

            def target_of(origin, i=i):
                return outs[i].at[origin]

            lines.append(line_sends(me, owners, source_of, target_of, send, recv, i))
        for step in range(owners):
            for i in range(count):
                line_step(step, lines[i], owners)
            if step == 0:
                for i in range(count):
                    copies.append(pltpu.make_async_copy(own[i], outs[i].at[me], local.at[i]))
                    copies[-1].start()
        for i in range(count):
            copies[i].wait()
            line_finish(lines[i], owners)

    return pl.pallas_call(
        kernel,
        out_shape=[jax.ShapeDtypeStruct((owners,) + b.shape, b.dtype) for b in blocks],
        in_specs=[vmem_spec()] * count,
        out_specs=[any_spec()] * count,
        scratch_shapes=[
            pltpu.SemaphoreType.DMA((count, 2, owners - 1)),
            pltpu.SemaphoreType.DMA((count, 2, owners - 1)),
            pltpu.SemaphoreType.DMA((count,)),
        ],
        compiler_params=kernel_params(collective),
    )(*blocks)


def add_rows(target, addend, chunk):
    @pl.loop(0, target.shape[0] // chunk)
    def _(index):
        rows = pl.ds(pl.multiple_of(index * chunk, chunk), chunk)
        target[rows, :] = (target[rows, :].astype(F32) + addend[rows, :].astype(F32)).astype(
            target.dtype
        )


def scatter_line(own, held, out, send, recv, me, owners, chunk):
    def copy(side, step, source):
        toward = 1 - 2 * side
        return pltpu.make_async_remote_copy(
            src_ref=source,
            dst_ref=held.at[side, step],
            send_sem=send.at[side, step],
            recv_sem=recv.at[side, step],
            device_id={"expert": me + toward},
            device_id_type=MESH,
        )

    def advance(step):
        for side in range(2):
            toward = 1 - 2 * side
            behind = me if side == 0 else owners - 1 - me
            block = own.at[me + toward * (owners - 1 - step)]

            @pl.when(behind == 0)
            def _():
                copy(side, step, block).start()

            if step > 0:
                before = held.at[side, step - 1]

                @pl.when((behind >= 1) & (behind <= step))
                def _():
                    copy(side, step - 1, before).wait_recv()
                    add_rows(before, block, chunk)
                    copy(side, step, before).start()

    def finish():
        for side in range(2):
            behind = me if side == 0 else owners - 1 - me

            @pl.when(behind >= 1)
            def _():
                copy(side, owners - 2, held.at[side, owners - 2]).wait_recv()

        right, left = held.at[0, owners - 2], held.at[1, owners - 2]
        mine = own.at[me]

        @pl.loop(0, out.shape[0] // chunk)
        def _(index):
            rows = pl.ds(pl.multiple_of(index * chunk, chunk), chunk)
            total = mine[rows, :].astype(F32)
            zero = jnp.zeros_like(total)
            total = total + jnp.where(me > 0, right[rows, :].astype(F32), zero)
            total = total + jnp.where(me < owners - 1, left[rows, :].astype(F32), zero)
            out[rows, :] = total.astype(out.dtype)

        for side in range(2):
            behind = me if side == 0 else owners - 1 - me
            for step in range(owners - 1):

                @pl.when(behind <= step)
                def _():
                    copy(side, step, held.at[side, step]).wait_send()

    return advance, finish


def line_scratch(block, owners):
    return [
        pltpu.VMEM((2, owners - 1) + block.shape[1:], block.dtype),
        pltpu.SemaphoreType.DMA((2, owners - 1)),
        pltpu.SemaphoreType.DMA((2, owners - 1)),
    ]


def line_scatter(blocks, owners, collective):
    count = len(blocks)

    def kernel(*refs):
        own, outs, scratch = refs[:count], refs[count : 2 * count], refs[2 * count :]
        me = lax.axis_index("expert")
        greet_all(me, owners, 0, 0)
        lines = []
        for i in range(count):
            held, send, recv = scratch[3 * i : 3 * i + 3]
            lines.append(scatter_line(own[i], held, outs[i], send, recv, me, owners, 32))
        for step in range(owners - 1):
            for advance, _ in lines:
                advance(step)
        for _, finish in lines:
            finish()

    return pl.pallas_call(
        kernel,
        out_shape=[jax.ShapeDtypeStruct(b.shape[1:], F32) for b in blocks],
        in_specs=[vmem_spec()] * count,
        out_specs=[vmem_spec()] * count,
        scratch_shapes=[one for b in blocks for one in line_scratch(b, owners)],
        compiler_params=kernel_params(collective),
    )(*blocks)


def column_parts(width):
    middle = width // 2 // 128 * 128
    return ((0, middle), (middle, width))


def bit_order(part, bits):
    return list(range(1, bits)) if part == 0 else list(range(bits - 1, 0, -1))


def spread(out, place, start, stop):
    return out.at[tuple(place) + (slice(None), slice(start, stop))]


def fan_out(arrays, lead, dp_index, bits, send, recv, between=None):
    def copy(slot, ref, bit, known, start, stop):
        place = lead + [
            slice(None) if one in known else bit_of(dp_index, one)
            for one in range(bits - 1, -1, -1)
        ]
        view = ref.at[tuple(place) + (slice(None), slice(start, stop))]
        return pltpu.make_async_remote_copy(
            src_ref=view,
            dst_ref=view,
            send_sem=send.at[slot],
            recv_sem=recv.at[slot],
            device_id={"dp": partner_of(dp_index, bit)},
            device_id_type=MESH,
        )

    slot = 0
    for stage in range(bits):
        going = []
        for ref in arrays:
            if stage == bits - 1:
                going.append(copy(slot, ref, 0, set(range(1, bits)), 0, ref.shape[-1]))
                slot += 1
                continue
            for part, (start, stop) in enumerate(column_parts(ref.shape[-1])):
                order = bit_order(part, bits)
                going.append(
                    copy(slot, ref, order[stage], set(order[:stage]), start, stop)
                )
                slot += 1
        for one in going:
            one.start()
        for one in going:
            one.wait()
        if stage == bits - 2 and between is not None:
            between()


def reduce_all(grads, blocks, owners, dp_size, collective):
    bits = dp_size.bit_length() - 1
    shapes = [(g.shape[0] // (owners * dp_size), g.shape[1]) for g in grads]
    count, extra = len(grads), len(blocks)
    pieces = [
        (i, part, start, stop)
        for i, (_, width) in enumerate(shapes)
        for part, (start, stop) in enumerate(column_parts(width))
    ]
    many = len(pieces)

    def kernel(*refs):
        take = iter(refs)
        grad_refs = [next(take) for _ in range(count)]
        block_refs = [next(take) for _ in range(extra)]
        outs = [next(take) for _ in range(count)]
        block_outs = [next(take) for _ in range(extra)]
        pairs = [next(take) for _ in range(count)]
        held = [[next(take) for _ in range(many)] for _ in range(bits - 1)]
        small = [[next(take) for _ in range(3)] for _ in range(many)]
        large = [[next(take) for _ in range(3)] for _ in range(extra)]
        fold_send, fold_recv, fan_send, fan_recv = take
        me, dp_index = lax.axis_index("expert"), lax.axis_index("dp")
        greet_all(me, owners, dp_index, bits)
        lines = [
            scatter_line(block_refs[i], large[i][0], block_outs[i], *large[i][1:], me, owners, 32)
            for i in range(extra)
        ]
        pending = [0]

        def push_lines():
            step = pending[0]
            pending[0] += 1
            for advance, finish in lines:
                if step < owners - 1:
                    advance(step)
                elif step == owners - 1:
                    finish()

        def fold(slot, bit, source, target):
            return pltpu.make_async_remote_copy(
                src_ref=source,
                dst_ref=target,
                send_sem=fold_send.at[slot],
                recv_sem=fold_recv.at[slot],
                device_id={"dp": partner_of(dp_index, bit)},
                device_id_type=MESH,
            )

        def add_all(target, source_of):
            others = list(target.shape[1:-2])

            @pl.loop(0, owners)
            def _(z):
                for flat in range(math.prod(others)):
                    place, rest = [], flat
                    for size in reversed(others):
                        place.insert(0, rest % size)
                        rest //= size
                    index = (z,) + tuple(place)
                    target[index] = (
                        target[index].astype(F32) + source_of(z, place).astype(F32)
                    ).astype(target.dtype)

        mine = bit_of(dp_index, 0)
        going = []
        for i in range(count):
            source = grad_refs[i].at[(slice(None),) * bits + (1 - mine,)]
            going.append(fold(i, 0, source, pairs[i]))
            going[-1].start()
        push_lines()
        for i in range(count):
            going[i].wait()
            add_all(pairs[i], lambda z, place: grad_refs[i][(z,) + tuple(place) + (mine,)])
        state = []
        for i, part, start, stop in pieces:
            columns = slice(start, stop)
            state.append((pairs[i], columns, sorted(range(1, bits), reverse=True)))
        for stage in range(bits - 1):
            going = []
            for index, (i, part, start, stop) in enumerate(pieces):
                ref, columns, axes = state[index]
                bit = bit_order(part, bits)[stage]
                axis = axes.index(bit)
                view = (slice(None),) * (1 + axis) + (1 - bit_of(dp_index, bit),)
                view = view + (slice(None),) * (len(axes) - axis) + (columns,)
                target = held[stage][index]
                one = fold(count + stage * many + index, bit, ref.at[view], target)
                one.start()
                going.append((one, target, ref, axis, bit, columns, axes))
            for index, (one, target, ref, axis, bit, columns, axes) in enumerate(going):
                one.wait()
                keep = bit_of(dp_index, bit)

                def source_of(z, place):
                    where = (z,) + tuple(place[:axis]) + (keep,) + tuple(place[axis:])
                    return ref[where + (slice(None), columns)]

                add_all(target, source_of)
                state[index] = (target, slice(None), [a for a in axes if a != bit])
            if stage == 0:
                push_lines()

        place = tuple(bit_of(dp_index, bit) for bit in range(bits - 1, -1, -1))
        short = []
        for index, (i, part, start, stop) in enumerate(pieces):
            rows = shapes[i][0]
            target = outs[i].at[place + (slice(None), slice(start, stop))]
            short.append(
                scatter_line(
                    state[index][0], small[index][0], target, *small[index][1:], me, owners, rows
                )
            )
        for step in range(owners - 1):
            for advance, _ in short:
                advance(step)
        for _, finish in short:
            finish()
        push_lines()
        fan_out(outs, [], dp_index, bits, fan_send, fan_recv)
        while pending[0] < owners:
            push_lines()

    scratch = []
    for rows, width in shapes:
        scratch.append(pltpu.VMEM((owners,) + (2,) * (bits - 1) + (rows, width), BF16))
    for stage in range(bits - 1):
        for i, part, start, stop in pieces:
            scratch.append(
                pltpu.VMEM(
                    (owners,) + (2,) * (bits - 2 - stage) + (shapes[i][0], stop - start), BF16
                )
            )
    for i, part, start, stop in pieces:
        block = jax.ShapeDtypeStruct((owners, shapes[i][0], stop - start), BF16)
        scratch += line_scratch(block, owners)
    for block in blocks:
        scratch += line_scratch(block, owners)
    folds = count + (bits - 1) * many
    fans = count + (bits - 1) * many
    scratch += [pltpu.SemaphoreType.DMA((folds,))] * 2 + [pltpu.SemaphoreType.DMA((fans,))] * 2
    operands = [
        g.reshape((owners,) + (2,) * bits + shape) for g, shape in zip(grads, shapes)
    ] + list(blocks)
    results = pl.pallas_call(
        kernel,
        out_shape=[jax.ShapeDtypeStruct((2,) * bits + shape, BF16) for shape in shapes]
        + [jax.ShapeDtypeStruct(b.shape[1:], F32) for b in blocks],
        in_specs=[vmem_spec()] * len(operands),
        out_specs=[vmem_spec()] * len(operands),
        scratch_shapes=scratch,
        compiler_params=kernel_params(collective),
    )(*operands)
    sums = [
        r.reshape(dp_size * rows, width) for r, (rows, width) in zip(results, shapes)
    ]
    return sums, results[count:]


def stream_sides(stream, block, me, owners, send, recv):
    def source_of(step, origin):
        return block if step == 0 else stream.at[origin]

    return line_sends(me, owners, source_of, lambda origin: stream.at[origin], send, recv, 0)


def stream_start(step, sides, owners):
    for behind, copy in sides:

        @pl.when((behind >= step) & (behind < owners - 1))
        def _():
            copy(step).start()


def stream_arrive(step, sides):
    for behind, copy in sides:

        @pl.when(behind >= step + 1)
        def _():
            copy(step).wait_recv()


def stream_sent(step, sides, owners):
    for behind, copy in sides:

        @pl.when((behind >= step) & (behind < owners - 1))
        def _():
            copy(step).wait_send()


def line_semaphores(owners):
    return [pltpu.SemaphoreType.DMA((1, 2, owners - 1)), pltpu.SemaphoreType.DMA((1, 2, owners - 1))]


def gather_rows(piece, block, owners, dp_size, collective):
    bits = dp_size.bit_length() - 1
    rows, width = piece.shape[0] // dp_size, piece.shape[1]
    shape = (owners,) + (2,) * bits + (rows, width)

    def kernel(piece_ref, block_ref, out, stream, *scratch):
        line_send, line_recv, stream_send, stream_recv, fan_send, fan_recv, local = scratch
        me, dp_index = lax.axis_index("expert"), lax.axis_index("dp")
        greet_all(me, owners, dp_index, bits)
        place = tuple(bit_of(dp_index, bit) for bit in range(bits - 1, -1, -1))
        mine = piece_ref.at[place]

        def source_of(step, origin):
            return mine if step == 0 else out.at[(origin,) + place]

        def target_of(origin):
            return out.at[(origin,) + place]

        sides = line_sends(me, owners, source_of, target_of, line_send, line_recv, 0)
        far = stream_sides(stream, block_ref, me, owners, stream_send, stream_recv)
        keep = pltpu.make_async_copy(mine, out.at[(me,) + place], local.at[0])
        stay = pltpu.make_async_copy(block_ref, stream.at[me], local.at[1])
        for step in range(owners):
            line_step(step, sides, owners)
            if step == 0:
                keep.start()
        stream_start(0, far, owners)
        stay.start()
        keep.wait()

        def between():
            stream_arrive(0, far)
            stream_start(1, far, owners)

        fan_out([out], [slice(None)], dp_index, bits, fan_send, fan_recv, between)
        line_finish(sides, owners)
        stay.wait()
        stream_sent(0, far, owners)
        stream_arrive(1, far)
        stream_sent(1, far, owners)

    full, stream = pl.pallas_call(
        kernel,
        out_shape=[
            jax.ShapeDtypeStruct(shape, BF16),
            jax.ShapeDtypeStruct((owners,) + block.shape, BF16),
        ],
        in_specs=[vmem_spec()] * 2,
        out_specs=[any_spec()] * 2,
        scratch_shapes=line_semaphores(owners)
        + line_semaphores(owners)
        + [
            pltpu.SemaphoreType.DMA((2 * bits - 1,)),
            pltpu.SemaphoreType.DMA((2 * bits - 1,)),
            pltpu.SemaphoreType.DMA((2,)),
        ],
        compiler_params=kernel_params(collective),
    )(piece.reshape((2,) * bits + (rows, width)), block)
    return full.reshape(owners * dp_size * rows, width), stream


def lane_below(shape, bound, period):
    return lax.rem(lax.broadcasted_iota(jnp.int32, shape, len(shape) - 1), period) < bound


def swing(values, cosine, sine):
    width = values.shape[1]
    half = HEAD_SIZE // 2
    front = lane_below(values.shape, half, HEAD_SIZE)
    other = jnp.where(
        front, -pltpu.roll(values, width - half, 1), pltpu.roll(values, half, 1)
    )
    times = width // 128
    return values * jnp.tile(cosine, (1, times)) + other * jnp.tile(sine, (1, times))


def contract(a, b, axis_a, axis_b):
    return lax.dot_general(
        a, b, (((axis_a,), (axis_b,)), ((), ())), preferred_element_type=F32
    )


def head_tiles(natural):
    front = lane_below(natural.shape, HEAD_SIZE, 128)
    wide = natural.astype(F32)
    turned = pltpu.roll(wide, HEAD_SIZE, 1)
    return [
        jnp.where(front, wide, turned).astype(BF16),
        natural,
        jnp.where(front, turned, wide).astype(BF16),
    ]


def masked_weights(query, key, start, stop, length, scale_factor):
    scores = contract(query, key[:stop], 1, 1) * scale_factor
    rows = start + lax.broadcasted_iota(jnp.int32, scores.shape, 0)
    columns = lax.broadcasted_iota(jnp.int32, scores.shape, 1)
    scores = jnp.where((columns <= rows) & (columns < length), scores, MASKED)
    exponent = jnp.exp(scores - jnp.max(scores, -1, keepdims=True))
    return exponent / jnp.sum(exponent, -1, keepdims=True)


def row_tiles(length):
    size = 256 if length % 256 == 0 else length
    return [(start, start + size) for start in range(0, length, size)]


def attention_forward(projected_ref, cosine_ref, sine_ref, length, rotated_ref, attended_ref, pair):
    scale_factor = HEAD_SIZE ** (-0.5)
    count = projected_ref.shape[0]
    query_width = QUERY_HEADS * HEAD_SIZE
    key_width = KEY_VALUE_HEADS * HEAD_SIZE

    def columns(start, width):
        return pl.ds(pl.multiple_of(start + pair * width, 128), width)

    cosine, sine = cosine_ref[...], sine_ref[...]
    query_at, key_at = columns(0, 384), columns(query_width, 128)
    value_at = columns(query_width + key_width, 128)
    query = swing(projected_ref[:, query_at], cosine, sine).astype(BF16)
    key = swing(projected_ref[:, key_at], cosine, sine).astype(BF16)
    value = projected_ref[:, value_at].astype(BF16)
    rotated_ref[:, query_at] = query
    rotated_ref[:, key_at] = key
    rotated_ref[:, value_at] = value
    keys, values = head_tiles(key), head_tiles(value)
    for tile in range(3):
        for start, stop in row_tiles(count):
            both = query[start:stop, tile * 128 : tile * 128 + 128]
            front = lane_below(both.shape, HEAD_SIZE, 128)
            parts = []
            for side in range(2):
                one = jnp.where(front == (side == 0), both, jnp.zeros_like(both))
                weights = masked_weights(one, keys[tile], start, stop, length, scale_factor)
                parts.append(contract(weights.astype(BF16), values[tile][:stop], 1, 0))
            attended_ref[start:stop, columns_of(pair, tile)] = jnp.where(
                front, parts[0], parts[1]
            ).astype(BF16)


def columns_of(pair, tile):
    return pl.ds(pl.multiple_of(pair * 384 + tile * 128, 128), 128)


def attention_backward(rotated_ref, grad_ref, cosine_ref, sine_ref, length, out_ref, pair):
    scale_factor = HEAD_SIZE ** (-0.5)
    count = rotated_ref.shape[0]
    query_width = QUERY_HEADS * HEAD_SIZE
    key_width = KEY_VALUE_HEADS * HEAD_SIZE

    def columns(start, width):
        return pl.ds(pl.multiple_of(start + pair * width, 128), width)

    cosine, sine = cosine_ref[...], sine_ref[...]
    key_at = columns(query_width, 128)
    value_at = columns(query_width + key_width, 128)
    keys, values = head_tiles(rotated_ref[:, key_at]), head_tiles(rotated_ref[:, value_at])
    front = lane_below((count, 128), HEAD_SIZE, 128)
    key_total = value_total = None
    for tile in range(3):
        key_sum = jnp.zeros((count, 128), F32)
        value_sum = jnp.zeros((count, 128), F32)
        for start, stop in row_tiles(count):
            query = rotated_ref[start:stop, columns_of(pair, tile)]
            grad = grad_ref[start:stop, columns_of(pair, tile)]
            part = front[start:stop]
            parts = []
            for side in range(2):
                chosen = part == (side == 0)
                one = jnp.where(chosen, query, jnp.zeros_like(query))
                rise = jnp.where(chosen, grad, jnp.zeros_like(grad))
                weights = masked_weights(one, keys[tile], start, stop, length, scale_factor)
                weight_grad = contract(rise, values[tile][:stop], 1, 1)
                score_grad = (
                    weights
                    * (weight_grad - jnp.sum(weights * weight_grad, -1, keepdims=True))
                ).astype(BF16)
                parts.append(contract(score_grad, keys[tile][:stop], 1, 0))
                key_part = contract(score_grad, one, 0, 0)
                value_part = contract(weights.astype(BF16), rise, 0, 0)
                if stop < count:
                    rest = jnp.zeros((count - stop, 128), F32)
                    key_part = jnp.concatenate([key_part, rest], 0)
                    value_part = jnp.concatenate([value_part, rest], 0)
                key_sum = key_sum + key_part
                value_sum = value_sum + value_part
            query_grad = jnp.where(part, parts[0], parts[1]) * scale_factor
            out_ref[start:stop, columns_of(pair, tile)] = swing(
                query_grad, cosine[start:stop], -sine[start:stop]
            ).astype(BF16)
        sums = []
        for total in (key_sum, value_sum):
            if tile != 1:
                total = total + pltpu.roll(total, HEAD_SIZE, 1)
                total = jnp.where(front == (tile == 0), total, jnp.zeros_like(total))
            sums.append(total)
        key_total = sums[0] if key_total is None else key_total + sums[0]
        value_total = sums[1] if value_total is None else value_total + sums[1]
    out_ref[:, key_at] = swing(key_total * scale_factor, cosine, -sine).astype(BF16)
    out_ref[:, value_at] = value_total.astype(BF16)


def angle_tables(length):
    cosine, sine = tables(length, HEAD_SIZE)
    return jnp.tile(cosine, (1, 4)), jnp.tile(sine, (1, 4))


def smem_spec():
    return pl.BlockSpec(memory_space=pltpu.SMEM)


def local_params():
    return pltpu.CompilerParams(vmem_limit_bytes=VMEM_LIMIT)


def attend_backward(rotated, grad, cosine, sine, length):
    count, width = rotated.shape

    def kernel(length_ref, rotated_ref, grad_ref, cosine_ref, sine_ref, out_ref):
        @pl.loop(0, KEY_VALUE_HEADS // 2)
        def _(pair):
            attention_backward(
                rotated_ref, grad_ref, cosine_ref, sine_ref, length_ref[0], out_ref, pair
            )

        out_ref[:, width:] = jnp.zeros((count, AUX), BF16)

    return pl.pallas_call(
        kernel,
        out_shape=jax.ShapeDtypeStruct((count, width + AUX), BF16),
        in_specs=[smem_spec()] + [vmem_spec()] * 4,
        out_specs=vmem_spec(),
        compiler_params=local_params(),
    )(length, rotated, grad, cosine, sine)


def attend_forward(projected, cosine, sine, length, width, stream, owners, collective):
    count = projected.shape[0]

    def kernel(length_ref, projected_ref, cosine_ref, sine_ref, _, *refs):
        rotated_ref, attended_ref, stream_ref, send, recv = refs
        me = lax.axis_index("expert")
        greet_all(me, owners, 0, 0)
        far = stream_sides(stream_ref, None, me, owners, send, recv)
        stream_start(2, far, owners)

        @pl.loop(0, KEY_VALUE_HEADS // 2)
        def _(pair):
            attention_forward(
                projected_ref, cosine_ref, sine_ref, length_ref[0], rotated_ref, attended_ref, pair
            )

        for step in range(3, owners - 1):
            stream_arrive(step - 1, far)
            stream_start(step, far, owners)
        stream_arrive(owners - 2, far)
        for step in range(2, owners - 1):
            stream_sent(step, far, owners)

    return pl.pallas_call(
        kernel,
        out_shape=[
            jax.ShapeDtypeStruct((count, width), BF16),
            jax.ShapeDtypeStruct((count, QUERY_HEADS * HEAD_SIZE), BF16),
            jax.ShapeDtypeStruct(stream.shape, BF16),
        ],
        in_specs=[smem_spec()] + [vmem_spec()] * 3 + [any_spec()],
        out_specs=[vmem_spec()] * 2 + [any_spec()],
        scratch_shapes=line_semaphores(owners),
        input_output_aliases={4: 2},
        compiler_params=kernel_params(collective),
    )(length, projected, cosine, sine, stream)


def gather_slow(piece, dp_index, dp_size):
    rows = piece.shape[0] // dp_size
    part = lax.dynamic_slice_in_dim(piece, dp_index * rows, rows, 0)
    return lax.all_gather(part, ("expert", "dp"), axis=0, tiled=True)


def per_device(
    tokens,
    seq_lengths,
    routes,
    norm_attn,
    query_key_value_weight,
    w_out,
    norm_moe,
    router,
    expert_in,
    expert_out,
    cotangent,
):
    owners = lax.axis_size("expert")
    dp_size = lax.axis_size("dp")
    owner = lax.axis_index("expert")
    dp_index = lax.axis_index("dp")
    _, length, width = tokens.shape
    local_experts = expert_in.shape[0]
    experts = local_experts * owners
    capacity = length * TOPK // experts
    qkv_width = (QUERY_HEADS + 2 * KEY_VALUE_HEADS) * HEAD_SIZE

    small = jnp.concatenate(
        [
            router,
            norm_attn[:, None],
            norm_moe[:, None],
            jnp.zeros((router.shape[0], AUX - experts - 2), BF16),
        ],
        1,
    )
    qkv_packed, stream = gather_rows(
        jnp.concatenate([query_key_value_weight, small], 1), cotangent[0], owners, dp_size, 1
    )
    out_full = gather_slow(w_out, dp_index, dp_size)
    small_full = qkv_packed[:, qkv_width:].astype(F32)
    router_wide = small_full[:, :experts]
    gain_first = small_full[:, experts]
    gain_second = small_full[:, experts + 1]

    sequence_live = seq_lengths[0]
    position = jnp.arange(length)
    live = position < sequence_live
    live_rows = live[:, None].astype(F32)
    inputs = tokens[0].astype(F32)
    normed_first, factor_first = norm_apply(inputs, gain_first)
    normed_low = normed_first.astype(BF16)
    projected_rows = dot("td,df->tf", normed_low, qkv_packed)
    cosine, sine_table = angle_tables(length)
    rotated, attended, upstream_all = attend_forward(
        projected_rows, cosine, sine_table, seq_lengths, qkv_width, stream, owners, 6
    )
    hidden_sum = inputs + dot("ti,id->td", attended, out_full)
    normed_second, factor_second = norm_apply(hidden_sum, gain_second)
    second_low = normed_second.astype(BF16)

    chosen = jnp.any(routes[0][:, :, None] == jnp.arange(experts)[None, None, :], 1)
    pairs = chosen & live[:, None]
    earlier = (position[:, None] > position[None, :]).astype(BF16)
    ranking = dot("tu,ue->te", earlier, pairs.astype(BF16))
    kept = pairs & (ranking < capacity)
    logits = jnp.dot(second_low.astype(F32), router_wide, precision=PRECISE)
    topmost = jnp.max(jnp.where(chosen, logits, -jnp.inf), -1, keepdims=True)
    exponent = jnp.where(chosen, jnp.exp(jnp.where(chosen, logits - topmost, 0.0)), 0.0)
    gating = exponent / jnp.sum(exponent, -1, keepdims=True)
    kept_weight = jnp.where(kept, gating, 0.0)
    slot_of = jnp.where(kept, ranking, -1.0).astype(BF16)
    weight_high, weight_low = split_two(kept_weight)
    extra = jnp.concatenate(
        [slot_of, weight_high, weight_low, jnp.zeros((length, AUX - 3 * experts), BF16)], 1
    )
    rows_all, extra_all = line_gather([second_low, extra], owners, 2)
    extra_all = extra_all.astype(F32)

    def own(column):
        return lax.dynamic_slice_in_dim(
            extra_all, column * experts + owner * local_experts, local_experts, 2
        )

    slots = own(0)
    weights_all = own(1) + own(2)
    hits = slots.transpose(0, 2, 1)[:, :, None, :] == jnp.arange(capacity, dtype=F32)[:, None]
    picks = hits.astype(BF16)
    slot_weight = jnp.sum(
        jnp.where(hits, weights_all.transpose(0, 2, 1)[:, :, None, :], 0.0), -1
    )
    inner_full = lax.all_gather(expert_in, "dp", axis=1, tiled=True)
    down_full = lax.all_gather(expert_out, "dp", axis=1, tiled=True)
    hidden_width = down_full.shape[1]

    rows_in = dot("sect,std->escd", picks, rows_all).astype(BF16)
    grad_in = dot("sect,std->escd", picks, upstream_all).astype(BF16)
    gate_up = dot("escd,edf->escf", rows_in, inner_full)
    gate_part = gate_up[..., :hidden_width]
    up_part = gate_up[..., hidden_width:]
    sigmoid_part = jax.nn.sigmoid(gate_part)
    activated = gate_part * sigmoid_part
    hidden = activated * up_part
    weight_column = slot_weight.transpose(1, 0, 2)[..., None]
    hidden_weighted = (hidden * weight_column).astype(BF16)
    hidden_grad = dot("escd,ehd->esch", grad_in, down_full)
    gate_grad_slot = jnp.sum(hidden.astype(BF16).astype(F32) * hidden_grad, -1)
    hidden_grad = hidden_grad * weight_column
    gate_part_grad = hidden_grad * up_part * sigmoid_part * (1.0 + gate_part * (1.0 - sigmoid_part))
    up_grad = hidden_grad * activated
    gate_up_grad = jnp.concatenate([gate_part_grad, up_grad], -1).astype(BF16)
    row_grad = dot("escf,edf->escd", gate_up_grad, inner_full).astype(BF16)
    back = dot("sect,escd->std", picks, row_grad).astype(BF16)
    gate_grad_own = jnp.sum(
        jnp.where(hits, gate_grad_slot.transpose(1, 0, 2)[..., None], 0.0), 2
    ).transpose(0, 2, 1)
    gate_wide = jnp.zeros((owners, length, experts), F32)
    gate_wide = lax.dynamic_update_slice_in_dim(gate_wide, gate_grad_own, owner * local_experts, 2)
    gate_packed = jnp.concatenate(
        list(split_two(gate_wide)) + [jnp.zeros((owners, length, AUX - 2 * experts), BF16)], 2
    )
    inner_weight_grad = dot("escd,escf->edf", rows_in, gate_up_grad).astype(BF16)
    down_weight_grad = dot("esch,escd->ehd", hidden_weighted, grad_in).astype(BF16)
    back, inner_weight_grad, down_weight_grad = lax.optimization_barrier(
        (back, inner_weight_grad, down_weight_grad)
    )
    inner_sum = lax.psum_scatter(
        inner_weight_grad, "dp", scatter_dimension=1, tiled=True
    ).astype(F32)
    down_sum = lax.psum_scatter(
        down_weight_grad, "dp", scatter_dimension=1, tiled=True
    ).astype(F32)
    back_sum, gate_sum = line_scatter([back, gate_packed], owners, 3)
    back_sum, hidden_late = lax.optimization_barrier((back_sum, hidden_weighted))
    expert_rows = dot("esch,ehd->escd", hidden_late, down_full).astype(BF16)
    mixed = dot("sect,escd->std", picks, expert_rows).astype(BF16)

    upstream = cotangent[0].astype(F32) * live_rows
    gate_grad = gate_sum[:, :experts] + gate_sum[:, experts : 2 * experts]
    logit_grad = gating * (gate_grad - jnp.sum(gating * gate_grad, -1, keepdims=True))
    second_grad = back_sum + jnp.dot(
        logit_grad, router_wide.T, precision=PRECISE
    )
    router_grad = jnp.dot(second_low.astype(F32).T, logit_grad, precision=PRECISE)
    hidden_back, gain_two_grad = norm_back(hidden_sum, factor_second, gain_second, second_grad)
    total_grad = upstream + hidden_back
    total_low = total_grad.astype(BF16)
    out_weight_grad = dot("ti,td->id", attended, total_low)
    attended_grad = dot("td,id->ti", total_low, out_full).astype(BF16)
    projected_grad = attend_backward(rotated, attended_grad, cosine, sine_table, seq_lengths)
    qkv_weight_grad = dot("td,tf->df", normed_low, projected_grad)
    first_grad = dot("tf,df->td", projected_grad, qkv_packed)
    input_back, gain_one_grad = norm_back(inputs, factor_first, gain_first, first_grad)
    input_grad = (total_grad + input_back).astype(BF16)
    small_grad = jnp.concatenate(
        [
            router_grad,
            gain_one_grad[:, None],
            gain_two_grad[:, None],
            jnp.zeros((width, AUX - experts - 2), F32),
        ],
        1,
    )
    packed_grad = lax.dynamic_update_slice(
        qkv_weight_grad.astype(BF16), small_grad.astype(BF16), (0, qkv_width)
    )
    grads = [packed_grad, out_weight_grad.astype(BF16)]
    if owners > 4:
        (packed_sum, out_sum), _ = reduce_all(grads, [], owners, dp_size, 4)
        (mixture,) = line_scatter([mixed], owners, 5)
    else:
        (packed_sum, out_sum), (mixture,) = reduce_all(grads, [mixed], owners, dp_size, 4)
    packed_sum = packed_sum.astype(F32)
    output = (live_rows * (hidden_sum + mixture)).astype(BF16)
    return (
        output[None],
        input_grad[None],
        packed_sum[:, qkv_width + experts],
        packed_sum[:, :qkv_width],
        out_sum.astype(F32),
        packed_sum[:, qkv_width + experts + 1],
        packed_sum[:, qkv_width : qkv_width + experts],
        inner_sum,
        down_sum,
    )


def solution(mesh):
    return jax.shard_map(
        per_device,
        mesh=mesh,
        in_specs=(
            P(("dp", "expert"), None, None),
            P(("dp", "expert")),
            P(("dp", "expert"), None, None),
            P("expert"),
            P("expert", None),
            P("expert", None),
            P("expert"),
            P("expert", None),
            P("expert", "dp", None),
            P("expert", "dp", None),
            P(("dp", "expert"), None, None),
        ),
        out_specs=(
            P(("dp", "expert"), None, None),
            P(("dp", "expert"), None, None),
            P("expert"),
            P("expert", None),
            P("expert", None),
            P("expert"),
            P("expert", None),
            P("expert", "dp", None),
            P("expert", "dp", None),
        ),
        check_vma=False,
    )
```

```python
import math

import jax
import jax.numpy as jnp
from jax import lax
from jax.experimental import pallas as pl
from jax.experimental.pallas import tpu as pltpu
from jax.sharding import PartitionSpec as P

QUERY_HEADS = 24
KEY_VALUE_HEADS = 8
HEAD_SIZE = 64
TOPK = 8
AUX = 128

PRECISE = lax.Precision.HIGHEST
EPSILON = 1e-06
MASKED = -1000000000.0
F32 = jnp.float32
BF16 = jnp.bfloat16


def tables(length, head):
    half_width = head // 2
    frequency = jnp.exp(jnp.arange(half_width, dtype=F32) * (-math.log(10000.0) / half_width))
    angles = jnp.arange(length, dtype=F32)[:, None] * frequency[None, :]
    return (jnp.cos(angles), jnp.sin(angles))


def norm_apply(value_rows, gain_vec):
    factor = lax.rsqrt(jnp.mean(value_rows * value_rows, -1, keepdims=True) + EPSILON)
    return (value_rows * factor * gain_vec, factor)


def norm_back(value_rows, factor, gain_vec, incoming):
    unit_rows = value_rows * factor
    scaled = incoming * gain_vec
    gain_grad = jnp.sum(incoming * unit_rows, 0)
    return (
        factor * (scaled - unit_rows * jnp.mean(scaled * unit_rows, -1, keepdims=True)),
        gain_grad,
    )


def dot(spec, a, b):
    return jnp.einsum(spec, a, b, preferred_element_type=F32)


def split_two(values):
    high = values.astype(BF16)
    low = (values - high.astype(F32)).astype(BF16)
    return (high, low)


MESH = pl.DeviceIdType.MESH
VMEM_LIMIT = 60 * 1024 * 1024


def vmem_spec():
    return pl.BlockSpec(memory_space=pltpu.VMEM)


def any_spec():
    return pl.BlockSpec(memory_space=pl.ANY)


def kernel_params(collective):
    return pltpu.CompilerParams(
        collective_id=collective, has_side_effects=True, vmem_limit_bytes=VMEM_LIMIT
    )


def greet_all(me, owners, dp_index, bits):
    barrier = pltpu.get_barrier_semaphore()
    for bit in range(bits):
        pl.semaphore_signal(
            barrier, inc=1, device_id={"dp": partner_of(dp_index, bit)}, device_id_type=MESH
        )
    ends = (me > 0, me < owners - 1)
    for offset, there in zip((-1, 1), ends):

        @pl.when(there)
        def _():
            pl.semaphore_signal(
                barrier, inc=1, device_id={"expert": me + offset}, device_id_type=MESH
            )

    pl.semaphore_wait(barrier, bits + ends[0].astype(jnp.int32) + ends[1].astype(jnp.int32))


def bit_of(index, bit):
    return lax.rem(index // (1 << bit), 2)


def partner_of(index, bit):
    return index + (1 - 2 * bit_of(index, bit)) * (1 << bit)


def line_sends(me, owners, source_of, target_of, send, recv, slot):
    first = []
    for side in range(2):
        toward = 1 - 2 * side
        behind = me if side == 0 else owners - 1 - me

        def copy(step, side=side, toward=toward):
            origin = me - toward * step
            return pltpu.make_async_remote_copy(
                src_ref=source_of(step, origin),
                dst_ref=target_of(origin),
                send_sem=send.at[slot, side, step],
                recv_sem=recv.at[slot, side, step],
                device_id={"expert": me + toward},
                device_id_type=MESH,
            )

        first.append((behind, copy))
    return first


def line_step(step, sides, owners):
    for behind, copy in sides:
        if step > 0:

            @pl.when(behind >= step)
            def _():
                copy(step - 1).wait_recv()

        if step < owners - 1:

            @pl.when((behind >= step) & (behind < owners - 1))
            def _():
                copy(step).start()


def line_finish(sides, owners):
    for behind, copy in sides:
        for step in range(owners - 1):

            @pl.when((behind >= step) & (behind < owners - 1))
            def _():
                copy(step).wait_send()


def add_rows(target, addend, chunk):
    @pl.loop(0, target.shape[0] // chunk)
    def _(index):
        rows = pl.ds(pl.multiple_of(index * chunk, chunk), chunk)
        target[rows, :] = (target[rows, :].astype(F32) + addend[rows, :].astype(F32)).astype(
            target.dtype
        )


def scatter_line(own, held, out, send, recv, me, owners, chunk):
    def copy(side, step, source):
        toward = 1 - 2 * side
        return pltpu.make_async_remote_copy(
            src_ref=source,
            dst_ref=held.at[side, step],
            send_sem=send.at[side, step],
            recv_sem=recv.at[side, step],
            device_id={"expert": me + toward},
            device_id_type=MESH,
        )

    def advance(step):
        for side in range(2):
            toward = 1 - 2 * side
            behind = me if side == 0 else owners - 1 - me
            block = own.at[me + toward * (owners - 1 - step)]

            @pl.when(behind == 0)
            def _():
                copy(side, step, block).start()

            if step > 0:
                before = held.at[side, step - 1]

                @pl.when((behind >= 1) & (behind <= step))
                def _():
                    copy(side, step - 1, before).wait_recv()
                    add_rows(before, block, chunk)
                    copy(side, step, before).start()

    def finish():
        for side in range(2):
            behind = me if side == 0 else owners - 1 - me

            @pl.when(behind >= 1)
            def _():
                copy(side, owners - 2, held.at[side, owners - 2]).wait_recv()

        right, left = held.at[0, owners - 2], held.at[1, owners - 2]
        mine = own.at[me]

        @pl.loop(0, out.shape[0] // chunk)
        def _(index):
            rows = pl.ds(pl.multiple_of(index * chunk, chunk), chunk)
            total = mine[rows, :].astype(F32)
            zero = jnp.zeros_like(total)
            total = total + jnp.where(me > 0, right[rows, :].astype(F32), zero)
            total = total + jnp.where(me < owners - 1, left[rows, :].astype(F32), zero)
            out[rows, :] = total.astype(out.dtype)

        for side in range(2):
            behind = me if side == 0 else owners - 1 - me
            for step in range(owners - 1):

                @pl.when(behind <= step)
                def _():
                    copy(side, step, held.at[side, step]).wait_send()

    return advance, finish


def line_scratch(block, owners):
    return [
        pltpu.VMEM((2, owners - 1) + block.shape[1:], block.dtype),
        pltpu.SemaphoreType.DMA((2, owners - 1)),
        pltpu.SemaphoreType.DMA((2, owners - 1)),
    ]


def line_scatter(blocks, owners, collective):
    count = len(blocks)

    def kernel(*refs):
        own, outs, scratch = refs[:count], refs[count : 2 * count], refs[2 * count :]
        me = lax.axis_index("expert")
        greet_all(me, owners, 0, 0)
        lines = []
        for i in range(count):
            held, send, recv = scratch[3 * i : 3 * i + 3]
            chunk = math.gcd(32, own[i].shape[1])
            lines.append(scatter_line(own[i], held, outs[i], send, recv, me, owners, chunk))
        for step in range(owners - 1):
            for advance, _ in lines:
                advance(step)
        for _, finish in lines:
            finish()

    return pl.pallas_call(
        kernel,
        out_shape=[jax.ShapeDtypeStruct(b.shape[1:], F32) for b in blocks],
        in_specs=[vmem_spec()] * count,
        out_specs=[vmem_spec()] * count,
        scratch_shapes=[one for b in blocks for one in line_scratch(b, owners)],
        compiler_params=kernel_params(collective),
    )(*blocks)


def column_parts(width):
    middle = width // 2 // 128 * 128
    return ((0, middle), (middle, width))


def bit_order(part, bits):
    return list(range(1, bits)) if part == 0 else list(range(bits - 1, 0, -1))


def spread(out, place, start, stop):
    return out.at[tuple(place) + (slice(None), slice(start, stop))]


def fan_out(arrays, lead, dp_index, bits, send, recv, between=None):
    def copy(slot, ref, bit, known, start, stop):
        place = lead + [
            slice(None) if one in known else bit_of(dp_index, one)
            for one in range(bits - 1, -1, -1)
        ]
        view = ref.at[tuple(place) + (slice(None), slice(start, stop))]
        return pltpu.make_async_remote_copy(
            src_ref=view,
            dst_ref=view,
            send_sem=send.at[slot],
            recv_sem=recv.at[slot],
            device_id={"dp": partner_of(dp_index, bit)},
            device_id_type=MESH,
        )

    slot = 0
    for stage in range(bits):
        going = []
        for ref in arrays:
            if stage == bits - 1:
                going.append(copy(slot, ref, 0, set(range(1, bits)), 0, ref.shape[-1]))
                slot += 1
                continue
            for part, (start, stop) in enumerate(column_parts(ref.shape[-1])):
                order = bit_order(part, bits)
                going.append(
                    copy(slot, ref, order[stage], set(order[:stage]), start, stop)
                )
                slot += 1
        for one in going:
            one.start()
        for one in going:
            one.wait()
        if stage == bits - 2 and between is not None:
            between()


def reduce_all(grads, blocks, owners, dp_size, collective):
    bits = dp_size.bit_length() - 1
    shapes = [(g.shape[0] // (owners * dp_size), g.shape[1]) for g in grads]
    count, extra = len(grads), len(blocks)
    pieces = [
        (i, part, start, stop)
        for i, (_, width) in enumerate(shapes)
        for part, (start, stop) in enumerate(column_parts(width))
    ]
    many = len(pieces)

    def kernel(*refs):
        take = iter(refs)
        grad_refs = [next(take) for _ in range(count)]
        block_refs = [next(take) for _ in range(extra)]
        outs = [next(take) for _ in range(count)]
        block_outs = [next(take) for _ in range(extra)]
        pairs = [next(take) for _ in range(count)]
        held = [[next(take) for _ in range(many)] for _ in range(bits - 1)]
        small = [[next(take) for _ in range(3)] for _ in range(many)]
        large = [[next(take) for _ in range(3)] for _ in range(extra)]
        fold_send, fold_recv, fan_send, fan_recv = take
        me, dp_index = lax.axis_index("expert"), lax.axis_index("dp")
        greet_all(me, owners, dp_index, bits)
        lines = [
            scatter_line(block_refs[i], large[i][0], block_outs[i], *large[i][1:], me, owners, 32)
            for i in range(extra)
        ]
        pending = [0]

        def push_lines():
            step = pending[0]
            pending[0] += 1
            for advance, finish in lines:
                if step < owners - 1:
                    advance(step)
                elif step == owners - 1:
                    finish()

        def fold(slot, bit, source, target):
            return pltpu.make_async_remote_copy(
                src_ref=source,
                dst_ref=target,
                send_sem=fold_send.at[slot],
                recv_sem=fold_recv.at[slot],
                device_id={"dp": partner_of(dp_index, bit)},
                device_id_type=MESH,
            )

        def add_all(target, source_of):
            others = list(target.shape[1:-2])

            @pl.loop(0, owners)
            def _(z):
                for flat in range(math.prod(others)):
                    place, rest = [], flat
                    for size in reversed(others):
                        place.insert(0, rest % size)
                        rest //= size
                    index = (z,) + tuple(place)
                    target[index] = (
                        target[index].astype(F32) + source_of(z, place).astype(F32)
                    ).astype(target.dtype)

        mine = bit_of(dp_index, 0)
        going = []
        for i in range(count):
            source = grad_refs[i].at[(slice(None),) * bits + (1 - mine,)]
            going.append(fold(i, 0, source, pairs[i]))
            going[-1].start()
        push_lines()
        for i in range(count):
            going[i].wait()
            add_all(pairs[i], lambda z, place: grad_refs[i][(z,) + tuple(place) + (mine,)])
        state = []
        for i, part, start, stop in pieces:
            columns = slice(start, stop)
            state.append((pairs[i], columns, sorted(range(1, bits), reverse=True)))
        for stage in range(bits - 1):
            going = []
            for index, (i, part, start, stop) in enumerate(pieces):
                ref, columns, axes = state[index]
                bit = bit_order(part, bits)[stage]
                axis = axes.index(bit)
                view = (slice(None),) * (1 + axis) + (1 - bit_of(dp_index, bit),)
                view = view + (slice(None),) * (len(axes) - axis) + (columns,)
                target = held[stage][index]
                one = fold(count + stage * many + index, bit, ref.at[view], target)
                one.start()
                going.append((one, target, ref, axis, bit, columns, axes))
            for index, (one, target, ref, axis, bit, columns, axes) in enumerate(going):
                one.wait()
                keep = bit_of(dp_index, bit)

                def source_of(z, place):
                    where = (z,) + tuple(place[:axis]) + (keep,) + tuple(place[axis:])
                    return ref[where + (slice(None), columns)]

                add_all(target, source_of)
                state[index] = (target, slice(None), [a for a in axes if a != bit])
            if stage == 0:
                push_lines()

        place = tuple(bit_of(dp_index, bit) for bit in range(bits - 1, -1, -1))
        short = []
        for index, (i, part, start, stop) in enumerate(pieces):
            rows = shapes[i][0]
            target = outs[i].at[place + (slice(None), slice(start, stop))]
            short.append(
                scatter_line(
                    state[index][0], small[index][0], target, *small[index][1:], me, owners, rows
                )
            )
        for step in range(owners - 1):
            for advance, _ in short:
                advance(step)
        for _, finish in short:
            finish()
        push_lines()
        fan_out(outs, [], dp_index, bits, fan_send, fan_recv)
        while pending[0] < owners:
            push_lines()

    scratch = []
    for rows, width in shapes:
        scratch.append(pltpu.VMEM((owners,) + (2,) * (bits - 1) + (rows, width), BF16))
    for stage in range(bits - 1):
        for i, part, start, stop in pieces:
            scratch.append(
                pltpu.VMEM(
                    (owners,) + (2,) * (bits - 2 - stage) + (shapes[i][0], stop - start), BF16
                )
            )
    for i, part, start, stop in pieces:
        block = jax.ShapeDtypeStruct((owners, shapes[i][0], stop - start), BF16)
        scratch += line_scratch(block, owners)
    for block in blocks:
        scratch += line_scratch(block, owners)
    folds = count + (bits - 1) * many
    fans = count + (bits - 1) * many
    scratch += [pltpu.SemaphoreType.DMA((folds,))] * 2 + [pltpu.SemaphoreType.DMA((fans,))] * 2
    operands = [
        g.reshape((owners,) + (2,) * bits + shape) for g, shape in zip(grads, shapes)
    ] + list(blocks)
    results = pl.pallas_call(
        kernel,
        out_shape=[jax.ShapeDtypeStruct((2,) * bits + shape, BF16) for shape in shapes]
        + [jax.ShapeDtypeStruct(b.shape[1:], F32) for b in blocks],
        in_specs=[vmem_spec()] * len(operands),
        out_specs=[vmem_spec()] * len(operands),
        scratch_shapes=scratch,
        compiler_params=kernel_params(collective),
    )(*operands)
    sums = [
        r.reshape(dp_size * rows, width) for r, (rows, width) in zip(results, shapes)
    ]
    return sums, results[count:]


def stream_sides(stream, block, me, owners, send, recv):
    def source_of(step, origin):
        return block if step == 0 else stream.at[origin]

    return line_sends(me, owners, source_of, lambda origin: stream.at[origin], send, recv, 0)


def stream_start(step, sides, owners):
    for behind, copy in sides:

        @pl.when((behind >= step) & (behind < owners - 1))
        def _():
            copy(step).start()


def stream_arrive(step, sides):
    for behind, copy in sides:

        @pl.when(behind >= step + 1)
        def _():
            copy(step).wait_recv()


def stream_sent(step, sides, owners):
    for behind, copy in sides:

        @pl.when((behind >= step) & (behind < owners - 1))
        def _():
            copy(step).wait_send()


def line_semaphores(owners):
    return [pltpu.SemaphoreType.DMA((1, 2, owners - 1)), pltpu.SemaphoreType.DMA((1, 2, owners - 1))]


def gather_rows(piece, block, owners, dp_size, collective):
    bits = dp_size.bit_length() - 1
    rows, width = piece.shape[0] // dp_size, piece.shape[1]
    shape = (owners,) + (2,) * bits + (rows, width)

    def kernel(piece_ref, block_ref, out, stream, *scratch):
        line_send, line_recv, stream_send, stream_recv, fan_send, fan_recv, local = scratch
        me, dp_index = lax.axis_index("expert"), lax.axis_index("dp")
        greet_all(me, owners, dp_index, bits)
        place = tuple(bit_of(dp_index, bit) for bit in range(bits - 1, -1, -1))
        mine = piece_ref.at[place]

        def source_of(step, origin):
            return mine if step == 0 else out.at[(origin,) + place]

        def target_of(origin):
            return out.at[(origin,) + place]

        sides = line_sends(me, owners, source_of, target_of, line_send, line_recv, 0)
        far = stream_sides(stream, block_ref, me, owners, stream_send, stream_recv)
        keep = pltpu.make_async_copy(mine, out.at[(me,) + place], local.at[0])
        stay = pltpu.make_async_copy(block_ref, stream.at[me], local.at[1])
        for step in range(owners):
            line_step(step, sides, owners)
            if step == 0:
                keep.start()
        stream_start(0, far, owners)
        stay.start()
        keep.wait()

        def between():
            stream_arrive(0, far)
            stream_start(1, far, owners)

        fan_out([out], [slice(None)], dp_index, bits, fan_send, fan_recv, between)
        line_finish(sides, owners)
        stay.wait()
        stream_sent(0, far, owners)
        stream_arrive(1, far)
        stream_sent(1, far, owners)

    full, stream = pl.pallas_call(
        kernel,
        out_shape=[
            jax.ShapeDtypeStruct(shape, BF16),
            jax.ShapeDtypeStruct((owners,) + block.shape, BF16),
        ],
        in_specs=[vmem_spec()] * 2,
        out_specs=[any_spec()] * 2,
        scratch_shapes=line_semaphores(owners)
        + line_semaphores(owners)
        + [
            pltpu.SemaphoreType.DMA((2 * bits - 1,)),
            pltpu.SemaphoreType.DMA((2 * bits - 1,)),
            pltpu.SemaphoreType.DMA((2,)),
        ],
        compiler_params=kernel_params(collective),
    )(piece.reshape((2,) * bits + (rows, width)), block)
    return full.reshape(owners * dp_size * rows, width), stream


def lane_below(shape, bound, period):
    return lax.rem(lax.broadcasted_iota(jnp.int32, shape, len(shape) - 1), period) < bound


def swing(values, cosine, sine):
    width = values.shape[1]
    half = HEAD_SIZE // 2
    front = lane_below(values.shape, half, HEAD_SIZE)
    other = jnp.where(
        front, -pltpu.roll(values, width - half, 1), pltpu.roll(values, half, 1)
    )
    times = width // 128
    return values * jnp.tile(cosine, (1, times)) + other * jnp.tile(sine, (1, times))


def contract(a, b, axis_a, axis_b):
    return lax.dot_general(
        a, b, (((axis_a,), (axis_b,)), ((), ())), preferred_element_type=F32
    )


def head_tiles(natural):
    front = lane_below(natural.shape, HEAD_SIZE, 128)
    wide = natural.astype(F32)
    turned = pltpu.roll(wide, HEAD_SIZE, 1)
    return [
        jnp.where(front, wide, turned).astype(BF16),
        natural,
        jnp.where(front, turned, wide).astype(BF16),
    ]


def masked_weights(query, key, start, stop, length, scale_factor):
    scores = contract(query, key[:stop], 1, 1) * scale_factor
    rows = start + lax.broadcasted_iota(jnp.int32, scores.shape, 0)
    columns = lax.broadcasted_iota(jnp.int32, scores.shape, 1)
    scores = jnp.where((columns <= rows) & (columns < length), scores, MASKED)
    exponent = jnp.exp(scores - jnp.max(scores, -1, keepdims=True))
    return exponent / jnp.sum(exponent, -1, keepdims=True)


def row_tiles(length):
    size = 256 if length % 256 == 0 else length
    return [(start, start + size) for start in range(0, length, size)]


def attention_forward(projected_ref, cosine_ref, sine_ref, length, rotated_ref, attended_ref, pair):
    scale_factor = HEAD_SIZE ** (-0.5)
    count = projected_ref.shape[0]
    query_width = QUERY_HEADS * HEAD_SIZE
    key_width = KEY_VALUE_HEADS * HEAD_SIZE

    def columns(start, width):
        return pl.ds(pl.multiple_of(start + pair * width, 128), width)

    cosine, sine = cosine_ref[...], sine_ref[...]
    query_at, key_at = columns(0, 384), columns(query_width, 128)
    value_at = columns(query_width + key_width, 128)
    query = swing(projected_ref[:, query_at], cosine, sine).astype(BF16)
    key = swing(projected_ref[:, key_at], cosine, sine).astype(BF16)
    value = projected_ref[:, value_at].astype(BF16)
    rotated_ref[:, query_at] = query
    rotated_ref[:, key_at] = key
    rotated_ref[:, value_at] = value
    keys, values = head_tiles(key), head_tiles(value)
    for tile in range(3):
        for start, stop in row_tiles(count):
            both = query[start:stop, tile * 128 : tile * 128 + 128]
            front = lane_below(both.shape, HEAD_SIZE, 128)
            parts = []
            for side in range(2):
                one = jnp.where(front == (side == 0), both, jnp.zeros_like(both))
                weights = masked_weights(one, keys[tile], start, stop, length, scale_factor)
                parts.append(contract(weights.astype(BF16), values[tile][:stop], 1, 0))
            attended_ref[start:stop, columns_of(pair, tile)] = jnp.where(
                front, parts[0], parts[1]
            ).astype(BF16)


def columns_of(pair, tile):
    return pl.ds(pl.multiple_of(pair * 384 + tile * 128, 128), 128)


def attention_backward(rotated_ref, grad_ref, cosine_ref, sine_ref, length, out_ref, pair):
    scale_factor = HEAD_SIZE ** (-0.5)
    count = rotated_ref.shape[0]
    query_width = QUERY_HEADS * HEAD_SIZE
    key_width = KEY_VALUE_HEADS * HEAD_SIZE

    def columns(start, width):
        return pl.ds(pl.multiple_of(start + pair * width, 128), width)

    cosine, sine = cosine_ref[...], sine_ref[...]
    key_at = columns(query_width, 128)
    value_at = columns(query_width + key_width, 128)
    keys, values = head_tiles(rotated_ref[:, key_at]), head_tiles(rotated_ref[:, value_at])
    front = lane_below((count, 128), HEAD_SIZE, 128)
    key_total = value_total = None
    for tile in range(3):
        key_sum = jnp.zeros((count, 128), F32)
        value_sum = jnp.zeros((count, 128), F32)
        for start, stop in row_tiles(count):
            query = rotated_ref[start:stop, columns_of(pair, tile)]
            grad = grad_ref[start:stop, columns_of(pair, tile)]
            part = front[start:stop]
            parts = []
            for side in range(2):
                chosen = part == (side == 0)
                one = jnp.where(chosen, query, jnp.zeros_like(query))
                rise = jnp.where(chosen, grad, jnp.zeros_like(grad))
                weights = masked_weights(one, keys[tile], start, stop, length, scale_factor)
                weight_grad = contract(rise, values[tile][:stop], 1, 1)
                score_grad = (
                    weights
                    * (weight_grad - jnp.sum(weights * weight_grad, -1, keepdims=True))
                ).astype(BF16)
                parts.append(contract(score_grad, keys[tile][:stop], 1, 0))
                key_part = contract(score_grad, one, 0, 0)
                value_part = contract(weights.astype(BF16), rise, 0, 0)
                if stop < count:
                    rest = jnp.zeros((count - stop, 128), F32)
                    key_part = jnp.concatenate([key_part, rest], 0)
                    value_part = jnp.concatenate([value_part, rest], 0)
                key_sum = key_sum + key_part
                value_sum = value_sum + value_part
            query_grad = jnp.where(part, parts[0], parts[1]) * scale_factor
            out_ref[start:stop, columns_of(pair, tile)] = swing(
                query_grad, cosine[start:stop], -sine[start:stop]
            ).astype(BF16)
        sums = []
        for total in (key_sum, value_sum):
            if tile != 1:
                total = total + pltpu.roll(total, HEAD_SIZE, 1)
                total = jnp.where(front == (tile == 0), total, jnp.zeros_like(total))
            sums.append(total)
        key_total = sums[0] if key_total is None else key_total + sums[0]
        value_total = sums[1] if value_total is None else value_total + sums[1]
    out_ref[:, key_at] = swing(key_total * scale_factor, cosine, -sine).astype(BF16)
    out_ref[:, value_at] = value_total.astype(BF16)


def angle_tables(length):
    cosine, sine = tables(length, HEAD_SIZE)
    return jnp.tile(cosine, (1, 4)), jnp.tile(sine, (1, 4))


def smem_spec():
    return pl.BlockSpec(memory_space=pltpu.SMEM)


def local_params():
    return pltpu.CompilerParams(vmem_limit_bytes=VMEM_LIMIT)


def attend_backward(rotated, grad, cosine, sine, length):
    count, width = rotated.shape

    def kernel(length_ref, rotated_ref, grad_ref, cosine_ref, sine_ref, out_ref):
        @pl.loop(0, KEY_VALUE_HEADS // 2)
        def _(pair):
            attention_backward(
                rotated_ref, grad_ref, cosine_ref, sine_ref, length_ref[0], out_ref, pair
            )

        out_ref[:, width:] = jnp.zeros((count, AUX), BF16)

    return pl.pallas_call(
        kernel,
        out_shape=jax.ShapeDtypeStruct((count, width + AUX), BF16),
        in_specs=[smem_spec()] + [vmem_spec()] * 4,
        out_specs=vmem_spec(),
        compiler_params=local_params(),
    )(length, rotated, grad, cosine, sine)


def attend_forward(projected, cosine, sine, length, width, stream, owners, collective):
    count = projected.shape[0]

    def kernel(length_ref, projected_ref, cosine_ref, sine_ref, _, *refs):
        rotated_ref, attended_ref, stream_ref, send, recv = refs
        me = lax.axis_index("expert")
        greet_all(me, owners, 0, 0)
        far = stream_sides(stream_ref, None, me, owners, send, recv)
        stream_start(2, far, owners)

        @pl.loop(0, KEY_VALUE_HEADS // 2)
        def _(pair):
            attention_forward(
                projected_ref, cosine_ref, sine_ref, length_ref[0], rotated_ref, attended_ref, pair
            )

        for step in range(3, owners - 1):
            stream_arrive(step - 1, far)
            stream_start(step, far, owners)
        stream_arrive(owners - 2, far)
        for step in range(2, owners - 1):
            stream_sent(step, far, owners)

    return pl.pallas_call(
        kernel,
        out_shape=[
            jax.ShapeDtypeStruct((count, width), BF16),
            jax.ShapeDtypeStruct((count, QUERY_HEADS * HEAD_SIZE), BF16),
            jax.ShapeDtypeStruct(stream.shape, BF16),
        ],
        in_specs=[smem_spec()] + [vmem_spec()] * 3 + [any_spec()],
        out_specs=[vmem_spec()] * 2 + [any_spec()],
        scratch_shapes=line_semaphores(owners),
        input_output_aliases={4: 2},
        compiler_params=kernel_params(collective),
    )(length, projected, cosine, sine, stream)


def visit_of(visit, me, owners):
    left, right = me, owners - 1 - me
    both = jnp.minimum(left, right)
    paired = visit <= 2 * both
    distance = jnp.where(paired, (visit + 1) // 2, visit - both)
    odd = lax.rem(visit, 2) == 1
    toward_left = jnp.where(paired, odd, left > right)
    opens = jnp.where(paired, odd, True) & (visit > 0)
    source = jnp.where(toward_left, me - distance, me + distance)
    return jnp.where(visit == 0, me, source), distance, opens


def expert_pass(rows, extra, upstream, inner, down, owners, capacity, collective):
    length, width = rows.shape
    count, _, wide = inner.shape
    hidden_width = wide // 2
    experts = count * owners
    places = -(-capacity // 16) * 16
    gate_rows = -(-experts // 8) * 8

    def kernel(
        rows_ref, extra_ref, upstream_ref, inner_ref, down_ref,
        all_ref, rows_out, grad_out, gate_out, hidden_out, back_out, mixed_out, slope_ref,
        inner_v, down_v, block_v, grad_v, table, table_wide, picks, dx, yw,
        rows_s, grad_s, gate_s, hidden_s, back_s, mixed_s,
        line_send, line_recv, weight_sem, load_sem, save_sem, sum_sem, own_sem,
    ):
        me = lax.axis_index("expert")
        greet_all(me, owners, 0, 0)
        sources = ((extra_ref, table), (rows_ref, all_ref))
        lines = []
        for slot, (first, rest) in enumerate(sources):

            def source_of(step, origin, first=first, rest=rest):
                return first if step == 0 else rest.at[origin]

            lines.append(
                line_sends(
                    me, owners, source_of, lambda origin, rest=rest: rest.at[origin],
                    line_send, line_recv, slot,
                )
            )
        own = [
            pltpu.make_async_copy(first, rest.at[me], own_sem.at[slot])
            for slot, (first, rest) in enumerate(sources)
        ]
        for one in own:
            one.start()
        for sides in lines:
            line_step(0, sides, owners)

        def weights(e):
            return (
                pltpu.make_async_copy(inner_ref.at[e], inner_v.at[e], weight_sem.at[0, e]),
                pltpu.make_async_copy(down_ref.at[e], down_v.at[e], weight_sem.at[1, e]),
            )

        for e in range(count):
            for one in weights(e):
                one.start()
        slope_ref[...] = jnp.zeros(slope_ref.shape, F32)
        for one in own:
            one.wait()

        def saves(source, e, half):
            at = pl.ds(pl.multiple_of(source * places, 16), places)
            return [
                pltpu.make_async_copy(s.at[half], o.at[e, at], save_sem.at[i, half])
                for i, (s, o) in enumerate(
                    ((rows_s, rows_out), (grad_s, grad_out), (gate_s, gate_out), (hidden_s, hidden_out))
                )
            ]

        def sums(source):
            return [
                pltpu.make_async_copy(s, o.at[source], sum_sem.at[i])
                for i, (s, o) in enumerate(((back_s, back_out), (mixed_s, mixed_out)))
            ]

        @pl.loop(0, owners)
        def _(visit):
            source, distance, opens = visit_of(visit, me, owners)
            for step in range(1, owners):

                @pl.when(opens & (distance == step))
                def _():
                    for sides in lines:
                        line_step(step, sides, owners)

            loads = (
                pltpu.make_async_copy(all_ref.at[source], block_v, load_sem.at[0]),
                pltpu.make_async_copy(upstream_ref.at[source], grad_v, load_sem.at[1]),
            )
            for one in loads:
                one.start()
            table_wide[...] = table[source].astype(F32)
            for one in loads:
                one.wait()

            @pl.loop(0, count)
            def _(e):
                half = lax.rem(e, 2)
                expert = me * count + e
                slot = table_wide[pl.ds(expert, 1), :]
                weight = (
                    table_wide[pl.ds(experts + expert, 1), :]
                    + table_wide[pl.ds(2 * experts + expert, 1), :]
                )
                place = lax.broadcasted_iota(jnp.int32, (places, length), 0).astype(F32)
                hits = place == slot
                pick = hits.astype(BF16)
                column = jnp.sum(jnp.where(hits, weight, 0.0), -1, keepdims=True)
                at = pl.ds(pl.multiple_of(e * places, 16), places)
                picks[at, :] = pick

                @pl.when(visit == 0)
                def _():
                    for one in weights(e):
                        one.wait()

                @pl.when((visit > 0) | (e >= 2))
                def _():
                    for one in saves(source, e, half):
                        one.wait()

                row = contract(pick, block_v[...], 1, 0).astype(BF16)
                rows_s[half] = row
                grad = contract(pick, grad_v[...], 1, 0).astype(BF16)
                grad_s[half] = grad
                gate_up = contract(row, inner_v[e], 1, 0)
                slope = contract(grad, down_v[e], 1, 1)
                gate, up = gate_up[:, :hidden_width], gate_up[:, hidden_width:]
                sigmoid = 1.0 / (1.0 + jnp.exp(-gate))
                active = gate * sigmoid
                hidden = active * up
                gate_slope = jnp.sum(hidden * slope, -1, keepdims=True)
                slope_ref[source, pl.ds(expert, 1), :] = jnp.sum(
                    jnp.where(hits, gate_slope, 0.0), 0, keepdims=True
                )
                hidden = (hidden * column).astype(BF16)
                hidden_s[half] = hidden
                slope = slope * column
                gate_s[half, :, :hidden_width] = (
                    slope * up * sigmoid * (1.0 + gate * (1.0 - sigmoid))
                ).astype(BF16)
                gate_s[half, :, hidden_width:] = (slope * active).astype(BF16)
                dx[at, :] = contract(gate_s[half], inner_v[e], 1, 1).astype(BF16)
                yw[at, :] = contract(hidden, down_v[e], 1, 0).astype(BF16)
                for one in saves(source, e, half):
                    one.start()

            @pl.when(visit > 0)
            def _():
                for one in sums(source):
                    one.wait()

            back_s[...] = contract(picks[...], dx[...], 0, 0).astype(BF16)
            mixed_s[...] = contract(picks[...], yw[...], 0, 0).astype(BF16)
            for one in sums(source):
                one.start()

        for one in sums(0):
            one.wait()
        for half in range(2):
            for one in saves(0, 0, half):
                one.wait()
        for sides in lines:
            line_finish(sides, owners)

    total = owners * places
    shapes = [
        ((owners, length, width), BF16),
        ((count, total, width), BF16),
        ((count, total, width), BF16),
        ((count, total, wide), BF16),
        ((count, total, hidden_width), BF16),
        ((owners, length, width), BF16),
        ((owners, length, width), BF16),
        ((owners, gate_rows, length), F32),
    ]
    return pl.pallas_call(
        kernel,
        out_shape=[jax.ShapeDtypeStruct(*shape) for shape in shapes],
        in_specs=[vmem_spec()] * 2 + [any_spec()] * 3,
        out_specs=[any_spec()] * 7 + [vmem_spec()],
        scratch_shapes=[
            pltpu.VMEM(inner.shape, BF16),
            pltpu.VMEM(down.shape, BF16),
            pltpu.VMEM((length, width), BF16),
            pltpu.VMEM((length, width), BF16),
            pltpu.VMEM((owners, AUX, length), BF16),
            pltpu.VMEM((AUX, length), F32),
            pltpu.VMEM((count * places, length), BF16),
            pltpu.VMEM((count * places, width), BF16),
            pltpu.VMEM((count * places, width), BF16),
            pltpu.VMEM((2, places, width), BF16),
            pltpu.VMEM((2, places, width), BF16),
            pltpu.VMEM((2, places, wide), BF16),
            pltpu.VMEM((2, places, hidden_width), BF16),
            pltpu.VMEM((length, width), BF16),
            pltpu.VMEM((length, width), BF16),
            pltpu.SemaphoreType.DMA((2, 2, owners - 1)),
            pltpu.SemaphoreType.DMA((2, 2, owners - 1)),
            pltpu.SemaphoreType.DMA((2, count)),
            pltpu.SemaphoreType.DMA((2,)),
            pltpu.SemaphoreType.DMA((4, 2)),
            pltpu.SemaphoreType.DMA((2,)),
            pltpu.SemaphoreType.DMA((2,)),
        ],
        compiler_params=kernel_params(collective),
    )(rows, extra, upstream, inner, down)


def gather_slow(piece, dp_index, dp_size):
    rows = piece.shape[0] // dp_size
    part = lax.dynamic_slice_in_dim(piece, dp_index * rows, rows, 0)
    return lax.all_gather(part, ("expert", "dp"), axis=0, tiled=True)


def per_device(
    tokens,
    seq_lengths,
    routes,
    norm_attn,
    query_key_value_weight,
    w_out,
    norm_moe,
    router,
    expert_in,
    expert_out,
    cotangent,
):
    owners = lax.axis_size("expert")
    dp_size = lax.axis_size("dp")
    owner = lax.axis_index("expert")
    dp_index = lax.axis_index("dp")
    _, length, width = tokens.shape
    local_experts = expert_in.shape[0]
    experts = local_experts * owners
    capacity = length * TOPK // experts
    qkv_width = (QUERY_HEADS + 2 * KEY_VALUE_HEADS) * HEAD_SIZE

    small = jnp.concatenate(
        [
            router,
            norm_attn[:, None],
            norm_moe[:, None],
            jnp.zeros((router.shape[0], AUX - experts - 2), BF16),
        ],
        1,
    )
    qkv_packed, stream = gather_rows(
        jnp.concatenate([query_key_value_weight, small], 1), cotangent[0], owners, dp_size, 1
    )
    out_full = gather_slow(w_out, dp_index, dp_size)
    small_full = qkv_packed[:, qkv_width:].astype(F32)
    router_wide = small_full[:, :experts]
    gain_first = small_full[:, experts]
    gain_second = small_full[:, experts + 1]

    sequence_live = seq_lengths[0]
    position = jnp.arange(length)
    live = position < sequence_live
    live_rows = live[:, None].astype(F32)
    inputs = tokens[0].astype(F32)
    normed_first, factor_first = norm_apply(inputs, gain_first)
    normed_low = normed_first.astype(BF16)
    projected_rows = dot("td,df->tf", normed_low, qkv_packed)
    cosine, sine_table = angle_tables(length)
    rotated, attended, upstream_all = attend_forward(
        projected_rows, cosine, sine_table, seq_lengths, qkv_width, stream, owners, 6
    )
    hidden_sum = inputs + dot("ti,id->td", attended, out_full)
    normed_second, factor_second = norm_apply(hidden_sum, gain_second)
    second_low = normed_second.astype(BF16)

    chosen = jnp.any(routes[0][:, :, None] == jnp.arange(experts)[None, None, :], 1)
    pairs = chosen & live[:, None]
    earlier = (position[:, None] > position[None, :]).astype(BF16)
    ranking = dot("tu,ue->te", earlier, pairs.astype(BF16))
    kept = pairs & (ranking < capacity)
    logits = jnp.dot(second_low.astype(F32), router_wide, precision=PRECISE)
    topmost = jnp.max(jnp.where(chosen, logits, -jnp.inf), -1, keepdims=True)
    exponent = jnp.where(chosen, jnp.exp(jnp.where(chosen, logits - topmost, 0.0)), 0.0)
    gating = exponent / jnp.sum(exponent, -1, keepdims=True)
    kept_weight = jnp.where(kept, gating, 0.0)
    slot_of = jnp.where(kept, ranking, -1.0).astype(BF16)
    weight_high, weight_low = split_two(kept_weight)
    extra = jnp.concatenate(
        [slot_of, weight_high, weight_low, jnp.zeros((length, AUX - 3 * experts), BF16)], 1
    ).T
    down_full = lax.all_gather(expert_out, "dp", axis=1, tiled=True)
    inner_full = lax.all_gather(expert_in, "dp", axis=1, tiled=True)
    _, rows_in, grad_in, gate_up_grad, hidden_weighted, back, mixed, slopes = expert_pass(
        second_low, extra, upstream_all, inner_full, down_full, owners, capacity, 2
    )
    inner_weight_grad = dot("ecd,ecf->edf", rows_in, gate_up_grad).astype(BF16)
    down_weight_grad = dot("ech,ecd->ehd", hidden_weighted, grad_in).astype(BF16)
    back, inner_weight_grad, down_weight_grad = lax.optimization_barrier(
        (back, inner_weight_grad, down_weight_grad)
    )
    inner_sum = lax.psum_scatter(
        inner_weight_grad, "dp", scatter_dimension=1, tiled=True
    ).astype(F32)
    down_sum = lax.psum_scatter(
        down_weight_grad, "dp", scatter_dimension=1, tiled=True
    ).astype(F32)
    back_sum, slope_sum = line_scatter([back, slopes], owners, 3)

    upstream = cotangent[0].astype(F32) * live_rows
    gate_grad = slope_sum[:experts].T
    logit_grad = gating * (gate_grad - jnp.sum(gating * gate_grad, -1, keepdims=True))
    second_grad = back_sum + jnp.dot(
        logit_grad, router_wide.T, precision=PRECISE
    )
    router_grad = jnp.dot(second_low.astype(F32).T, logit_grad, precision=PRECISE)
    hidden_back, gain_two_grad = norm_back(hidden_sum, factor_second, gain_second, second_grad)
    total_grad = upstream + hidden_back
    total_low = total_grad.astype(BF16)
    out_weight_grad = dot("ti,td->id", attended, total_low)
    attended_grad = dot("td,id->ti", total_low, out_full).astype(BF16)
    projected_grad = attend_backward(rotated, attended_grad, cosine, sine_table, seq_lengths)
    qkv_weight_grad = dot("td,tf->df", normed_low, projected_grad)
    first_grad = dot("tf,df->td", projected_grad, qkv_packed)
    input_back, gain_one_grad = norm_back(inputs, factor_first, gain_first, first_grad)
    input_grad = (total_grad + input_back).astype(BF16)
    small_grad = jnp.concatenate(
        [
            router_grad,
            gain_one_grad[:, None],
            gain_two_grad[:, None],
            jnp.zeros((width, AUX - experts - 2), F32),
        ],
        1,
    )
    packed_grad = lax.dynamic_update_slice(
        qkv_weight_grad.astype(BF16), small_grad.astype(BF16), (0, qkv_width)
    )
    grads = [packed_grad, out_weight_grad.astype(BF16)]
    if owners > 4:
        (packed_sum, out_sum), _ = reduce_all(grads, [], owners, dp_size, 4)
        (mixture,) = line_scatter([mixed], owners, 5)
    else:
        (packed_sum, out_sum), (mixture,) = reduce_all(grads, [mixed], owners, dp_size, 4)
    packed_sum = packed_sum.astype(F32)
    output = (live_rows * (hidden_sum + mixture)).astype(BF16)
    return (
        output[None],
        input_grad[None],
        packed_sum[:, qkv_width + experts],
        packed_sum[:, :qkv_width],
        out_sum.astype(F32),
        packed_sum[:, qkv_width + experts + 1],
        packed_sum[:, qkv_width : qkv_width + experts],
        inner_sum,
        down_sum,
    )


def solution(mesh):
    return jax.shard_map(
        per_device,
        mesh=mesh,
        in_specs=(
            P(("dp", "expert"), None, None),
            P(("dp", "expert")),
            P(("dp", "expert"), None, None),
            P("expert"),
            P("expert", None),
            P("expert", None),
            P("expert"),
            P("expert", None),
            P("expert", "dp", None),
            P("expert", "dp", None),
            P(("dp", "expert"), None, None),
        ),
        out_specs=(
            P(("dp", "expert"), None, None),
            P(("dp", "expert"), None, None),
            P("expert"),
            P("expert", None),
            P("expert", None),
            P("expert"),
            P("expert", None),
            P("expert", "dp", None),
            P("expert", "dp", None),
        ),
        check_vma=False,
    )
```
